128 devices in a mesh: req: 32 (over y_hi, x, z), sub: 4 (over y_lo, core).
Axes of the slice: x: 4, y: 4 (y_hi: 2, y_lo: 2; y = y_hi * 2 + y_lo), z: 4, core: 2. Of those that a mesh axis runs over, the one named last changes fastest.
Arguments:
- tokens: bfloat16 [16384, 2048], P(('req', 'sub')), may hold values from -6 to 6
- attn_gain: float32 [2048], replicated, may hold values from 0.25 to 1.75
- w_query: bfloat16 [2048, 1536], replicated, may hold values from -0.125 to 0.125
- w_latent: bfloat16 [2048, 576], replicated, may hold values from -0.125 to 0.125
- latent_gain: float32 [512], replicated, may hold values from 0.25 to 1.75
- w_key_up: bfloat16 [8, 128, 512], replicated, may hold values from -0.5 to 0.5
- w_value_up: bfloat16 [8, 512, 128], replicated, may hold values from -0.25 to 0.25
- w_out: bfloat16 [1024, 2048], replicated, may hold values from -0.1875 to 0.1875
- moe_gain: float32 [2048], replicated, may hold values from 0.25 to 1.75
- w_gate: bfloat16 [128, 2048, 704], P(('req', 'sub')), may hold values from -0.125 to 0.125
- w_up: bfloat16 [128, 2048, 704], P(('req', 'sub')), may hold values from -0.125 to 0.125
- w_down: bfloat16 [128, 704, 2048], P(('req', 'sub')), may hold values from -0.15625 to 0.15625
- expert_ids: int32 [16384, 6], P(('req', 'sub')), may hold values from 0 to 63, all different within a row; in each aligned block of 128 rows (0 to 127, 128 to 255, ...) at most 16 rows name the same one
- gate_weights: float32 [16384, 6], P(('req', 'sub')), may hold values from 0.1 to 0.6
- lengths: int32 [32, 3], P('req'), may hold values from 1 to 256, 512 in all within a row
- slab_group: int32 [32], P('req'), may hold values from 0 to 3
- owners: int32 [4], replicated, may hold values from 0 to 31, as said below
- prefix_pool: bfloat16 [32, 1024, 576], P('req'), as said below
Outputs:
- hidden_out: bfloat16 [16384, 2048], P(('req', 'sub'))
- new_cache: bfloat16 [16384, 576], P(('req', 'sub'))
The draws below stay inside these ranges and needn't reach their ends.
Inputs may be any that keep to these rules, and one draw needn't show every extreme that they name: `expert_ids`: each row names 6 different experts; in each aligned block of 128 rows (the rows of one device) no expert is named by more than 16 rows, and in some block one expert is named by exactly 16 rows. Each slab's 3 lengths sum to 512, and its longest request has exactly half of 512 tokens. 4 distinct slots, among them slot 0 and slot 31; group g's cached prefix is prefix_pool[owners[g]]. `prefix_pool`: each row holds 512 latent entries followed by 64 rotary key entries.
All inputs are finite; a program needn't handle non-finite values.
Results may differ from the reference program's by a relative error of at most 0.013.
The reference program's roundings to bfloat16 on the way count: a program that leaves them out, or rounds other values in their place, can miss the bound.
Values may be sent and summed in bfloat16 or wider, within the bound.
No kernel may reach another device: no remote copies, remote signals or barrier semaphores. Data moves between devices by JAX's collectives and lax.ppermute only.
A program may use at most 128 MiB of HBM per device.

```python
import math
import jax
import jax.numpy as jnp
import numpy as np
from jax import lax

D = 2048
HEADS = 8
NOPE = 128
ROPE = 64
LAT = 512
VHEAD = 128
FFN = 1408
TOPK = 6
GROUPS = 4
PREFIX = 1024
REQ_SLAB = 3
TOK_DEV = 128
SLAB = 512
TOKENS = 16384
E = 64
CAP = 16
HALF = 704
N_REQ = 32


def draw_owners(key, part):
    pick_key = jax.random.fold_in(key, 21)
    order_key = jax.random.fold_in(key, 22)
    middle = jax.random.permutation(pick_key, N_REQ - 2)[:GROUPS - 2].astype(jnp.int32) + 1
    slots = jnp.concatenate([jnp.zeros((1,), jnp.int32), jnp.full((1,), N_REQ - 1, jnp.int32), middle])
    return jax.random.permutation(order_key, slots).astype(jnp.int32)


def draw_prefix_pool(key, part):
    base_key = jax.random.fold_in(key, 11)
    shape = (N_REQ, PREFIX, LAT + ROPE)
    values = jax.random.normal(base_key, shape, jnp.float32)
    return values.astype(jnp.bfloat16)


def touch_ends(entries, rng, smallest, high):
    index_at = [jax.random.randint(jax.random.fold_in(rng, axis), (), 0, length) for axis, length in enumerate(entries.shape)]
    widest = entries.shape.index(max(entries.shape))
    next_to = index_at[:widest] + [(index_at[widest] + 1) % entries.shape[widest]] + index_at[widest + 1:]
    return entries.at[tuple(index_at)].set(smallest).at[tuple(next_to)].set(high)


def block_scale(stream_key, dims, cuts, low, largest):
    factor_of = 1.0
    for position, parts in cuts:
        heights = jax.random.uniform(jax.random.fold_in(jax.random.fold_in(stream_key, 6), position), (parts,), jnp.float32, low / len(cuts), largest / len(cuts))
        factor_of = factor_of * jnp.repeat(jnp.exp(heights), dims[position] // parts).reshape((-1,) + (1,) * (len(dims) - 1 - position))
    return factor_of


def split_up(number_of, total, most, skew):
    loads = [(1 << 20) // math.isqrt(grade ** skew) + 1 for grade in range(2, number_of + 1)]
    rest, holding = total - most - (number_of - 1), [1] * (number_of - 1)
    while rest > 0:
        free = [i for i in range(number_of - 1) if holding[i] < most]
        pool, left = sum([loads[i] for i in free]), rest
        for i in free:
            addition = min(most - holding[i], max(1, left * loads[i] // pool), rest)
            holding[i] = holding[i] + addition
            rest = rest - addition
    return np.array([most] + holding)


def uneven(stream_key, number_of, total, limit, slope):
    if number_of == 2:
        one = jax.random.randint(stream_key, (), max(1, total - limit), min(limit, total - 1) + 1)
        return jnp.stack([one, total - one])
    tallies = jnp.asarray(split_up(number_of, total, limit, slope), jnp.int32)
    couples = (number_of - 1) // 2
    source_of, taker = tallies[1:1 + 2 * couples:2], tallies[2:2 + 2 * couples:2]
    margin = jnp.minimum(source_of - 1, limit - taker)
    passed = jax.random.randint(jax.random.fold_in(stream_key, 1), (couples,), 0, 1 << 20) % (margin + 1)
    tallies = tallies.at[1:1 + 2 * couples:2].set(source_of - passed).at[2:2 + 2 * couples:2].set(taker + passed)
    return tallies[jax.random.permutation(jax.random.fold_in(stream_key, 2), number_of)]


def shared_out(own_key, own, number, rows, count, top, most, slope):
    order = jax.random.permutation(own_key, count)
    packed, ordinary = portions_of(count, rows * top, most, slope, True), portions_of(count, rows * top, most, slope, False)
    places = jnp.arange(count)

    def named(sizes, offset_by):
        used = int((sizes > 0).sum())
        fixed = max(1, used // 4)
        moved = fixed + (places - fixed + offset_by * (used - fixed)) % max(1, count - fixed)
        return jnp.zeros((count,), jnp.int32).at[order[jnp.where(places < fixed, places, moved)]].set(jnp.asarray(sizes, jnp.int32))

    sizes = jnp.where(number % 4 == 0, named(packed, number // 4), named(ordinary, number - number // 4 - 1))
    mixed = jax.random.permutation(jax.random.fold_in(own, 3), count)
    donor, receiver = mixed[0:count // 2 * 2:2], mixed[1:count // 2 * 2:2]
    margin = jnp.minimum(sizes[donor] - 1, most - sizes[receiver]) // 2
    margin = jnp.where((donor == order[0]) | (receiver == order[0]) | (sizes[receiver] == 0), 0, jnp.maximum(margin, 0))
    moved = jax.random.randint(jax.random.fold_in(own, 4), (count // 2,), 0, 1 << 20) % (margin + 1)
    sizes = sizes.at[donor].add(-moved).at[receiver].add(moved)
    members = jnp.searchsorted(jnp.cumsum(sizes), jnp.arange(rows * top), side="right").astype(jnp.int32)
    table = members.reshape(top, rows).T
    table = table[jax.random.permutation(jax.random.fold_in(own, 1), rows)]
    offset_by = jax.random.randint(jax.random.fold_in(own, 2), (rows, 1), 0, top)
    return jnp.take_along_axis(table, (jnp.arange(top)[None, :] + offset_by) % top, axis=1)


def portions_of(count, total, most, skew, full):
    weights = [(1 << 20) // math.isqrt(rank ** skew) + 1 for rank in range(1, count + 1)]
    largest = most if full else min(most, max(-(-total // count), total * weights[0] // sum(weights)))
    least = 1 if total - largest >= count - 1 else 0
    holding, rest = [largest] + [least] * (count - 1), total - largest - least * (count - 1)
    while rest > 0:
        movable = [i for i in range(1, count) if holding[i] < largest] or [i for i in range(1, count) if holding[i] < most]
        whole, left = sum([weights[i] for i in movable]), rest
        for i in movable:
            more = min(most - holding[i], max(1, left * weights[i] // whole), rest)
            holding[i] = holding[i] + more
            rest = rest - more
    return np.array(holding)


def gaussian(stream_key, shape, deviation, most, pieces=(), kind=jnp.bfloat16):
    loudness = block_scale(stream_key, shape, pieces, -0.22, 0.18) if pieces else 1.0
    entries = jax.random.normal(stream_key, shape, jnp.float32) * deviation * loudness
    return jnp.minimum(jnp.maximum(entries, -most), most).astype(kind)


def setup_inputs(seed: int = 0) -> dict:
    keys = jax.random.split(jax.random.key(seed), 19)
    tokens = gaussian(keys[0], (TOKENS, D), 1.0, 6.0, ((0, 128),))
    attn_gain = jnp.clip(1.0 + 0.15 * jax.random.normal(keys[1], (D,), jnp.float32), 0.25, 1.75)
    w_query = gaussian(keys[2], (D, HEADS * (NOPE + ROPE)), D ** -0.5, 0.125)
    w_latent = gaussian(keys[3], (D, LAT + ROPE), D ** -0.5, 0.125)
    latent_gain = jnp.clip(1.0 + 0.15 * jax.random.normal(keys[4], (LAT,), jnp.float32), 0.25, 1.75)
    w_key_up = gaussian(keys[5], (HEADS, NOPE, LAT), NOPE ** -0.5, 0.5)
    w_value_up = gaussian(keys[6], (HEADS, LAT, VHEAD), LAT ** -0.5, 0.25)
    w_out = gaussian(keys[7], (HEADS * VHEAD, D), (HEADS * VHEAD) ** -0.5, 0.1875)
    moe_gain = jnp.clip(1.0 + 0.15 * jax.random.normal(keys[8], (D,), jnp.float32), 0.25, 1.75)
    w_gate = gaussian(keys[9], (2 * E, D, HALF), D ** -0.5, 0.125, ((0, 128),))
    w_up = gaussian(keys[10], (2 * E, D, HALF), D ** -0.5, 0.125, ((0, 128),))
    w_down = gaussian(keys[11], (2 * E, HALF, D), FFN ** -0.5, 0.15625, ((0, 128),))
    expert_ids_keys = jax.random.split(jax.random.fold_in(keys[12], 1), TOKENS // TOK_DEV)
    expert_ids_turns = jax.random.permutation(jax.random.fold_in(keys[12], 3), TOKENS // TOK_DEV)
    expert_ids = jax.vmap(lambda own, number: shared_out(jax.random.fold_in(keys[12], 2), own, number, TOK_DEV, E, TOPK, CAP, 2))(expert_ids_keys, expert_ids_turns).reshape((TOKENS, TOPK))
    gate_weights = jnp.clip(0.1 + 0.5 * jax.random.uniform(keys[13], (TOKENS, TOPK), jnp.float32) ** block_scale(keys[13], (TOKENS, TOPK), ((0, 128),), -0.2, 0.2), 0.1, 0.6)
    lengths = jax.vmap(lambda own: uneven(own, REQ_SLAB, SLAB, SLAB // 2, 2))(jax.random.split(keys[14], N_REQ)).reshape((N_REQ, REQ_SLAB)).astype(jnp.int32)
    slab_group = touch_ends(jax.random.randint(keys[15], (N_REQ,), 0, GROUPS), jax.random.fold_in(keys[15], 1), 0, GROUPS - 1).astype(jnp.int32)
    owners = draw_owners(jax.random.fold_in(keys[18], 71), 0)
    prefix_pool = draw_prefix_pool(jax.random.fold_in(keys[18], 71), 0)
    return dict(tokens=tokens, attn_gain=attn_gain, w_query=w_query, w_latent=w_latent, latent_gain=latent_gain, w_key_up=w_key_up, w_value_up=w_value_up, w_out=w_out, moe_gain=moe_gain, w_gate=w_gate, w_up=w_up, w_down=w_down, expert_ids=expert_ids, gate_weights=gate_weights, lengths=lengths, slab_group=slab_group, owners=owners, prefix_pool=prefix_pool)


EPSILON = 1e-06

def rms_scale(values, gain):
    return values * lax.rsqrt(lax.optimization_barrier(jnp.mean(values * values, axis=-1, keepdims=True)) + EPSILON) * gain

def angle_tables(positions, rope_width):
    half_width = rope_width // 2
    inverse = 10000.0 ** (-jnp.arange(half_width, dtype=jnp.float32) / half_width)
    angles = positions.astype(jnp.float32)[:, None] * inverse[None, :]
    return (jnp.cos(angles), jnp.sin(angles))

def rotate(values, cos_part, sin_part):
    half_width = values.shape[-1] // 2
    first_half = values[..., :half_width]
    second = values[..., half_width:]
    return jnp.concatenate([first_half * cos_part - second * sin_part, second * cos_part + first_half * sin_part], axis=-1)

def slab_layout(req_lengths, slab_rows):
    req_ends = jnp.cumsum(req_lengths).astype(jnp.int32)
    req_starts = req_ends - req_lengths
    slab_pos = jnp.arange(slab_rows, dtype=jnp.int32)
    segment = lax.optimization_barrier(jnp.sum((slab_pos[:, None] >= req_ends[None, :]).astype(jnp.int32), axis=1))
    member_of = segment[:, None] == jnp.arange(req_lengths.shape[0], dtype=jnp.int32)[None, :]
    seg_start = lax.optimization_barrier(jnp.sum(jnp.where(member_of, req_starts[None, :], 0), axis=1)).astype(jnp.int32)
    return (slab_pos, segment, slab_pos - seg_start)

def reference(tokens, attn_gain, w_query, w_latent, latent_gain, w_key_up, w_value_up, w_out, moe_gain, w_gate, w_up, w_down, expert_ids, gate_weights, lengths, slab_group, owners, prefix_pool):
    score_scale = (NOPE + ROPE) ** (-0.5)

    def attend_slab(inputs):
        slab_tokens, req_lengths, group_id = inputs
        slab_pos, segment, offset = slab_layout(req_lengths, SLAB)
        cos_part, sin_part = angle_tables(PREFIX + offset, ROPE)
        normed = rms_scale(slab_tokens.astype(jnp.float32), attn_gain).astype(jnp.bfloat16)
        latent = jnp.dot(normed, w_latent, preferred_element_type=jnp.float32)
        cache_rows = jnp.concatenate([rms_scale(latent[:, :LAT], latent_gain), rotate(latent[:, LAT:], cos_part, sin_part)], axis=1).astype(jnp.bfloat16)
        queries = jnp.dot(normed, w_query, preferred_element_type=jnp.float32).astype(jnp.bfloat16)
        queries = lax.optimization_barrier(queries).reshape(SLAB, HEADS, NOPE + ROPE).astype(jnp.float32)
        query_lat = jnp.einsum('thj,hjc->thc', queries[:, :, :NOPE], w_key_up.astype(jnp.float32))
        query_rot = rotate(queries[:, :, NOPE:], cos_part[:, None, :], sin_part[:, None, :])
        query_full = jnp.concatenate([query_lat, query_rot], axis=2).astype(jnp.bfloat16)
        key_rows = jnp.concatenate([prefix_pool[owners[group_id]], cache_rows], axis=0)
        query_full, key_rows = lax.optimization_barrier((query_full, key_rows))
        key_float = key_rows.astype(jnp.float32)
        scores = jnp.einsum('thc,kc->thk', query_full.astype(jnp.float32), key_float) * score_scale
        causal = (segment[None, :] == segment[:, None]) & (slab_pos[None, :] <= slab_pos[:, None])
        allowed = jnp.concatenate([jnp.ones((SLAB, PREFIX), dtype=bool), causal], axis=1)
        scores = jnp.where(allowed[:, None, :], scores, -jnp.inf)
        row_top = lax.optimization_barrier(jnp.max(scores, axis=2, keepdims=True))
        weights = jnp.exp(scores - row_top)
        denominator = lax.optimization_barrier(jnp.sum(weights, axis=2, keepdims=True))
        rounded = lax.optimization_barrier(weights.astype(jnp.bfloat16)).astype(jnp.float32)
        latent_out = (jnp.einsum('thk,kc->thc', rounded, key_float[:, :LAT]) / denominator).astype(jnp.bfloat16)
        latent_out = lax.optimization_barrier(latent_out).astype(jnp.float32)
        head_out = jnp.einsum('thc,hcv->thv', latent_out, w_value_up.astype(jnp.float32)).astype(jnp.bfloat16).reshape(SLAB, HEADS * VHEAD)
        residual = slab_tokens.astype(jnp.float32) + jnp.dot(head_out, w_out, preferred_element_type=jnp.float32)
        normed_mid = rms_scale(residual, moe_gain).astype(jnp.bfloat16)
        return (residual, normed_mid, cache_rows)
    residual, normed_mid, cache_rows = lax.map(attend_slab, (tokens.reshape(N_REQ, SLAB, D), lengths, slab_group))
    residual = residual.reshape(TOKENS, D)
    normed_mid = normed_mid.reshape(TOKENS, D)
    new_cache = cache_rows.reshape(TOKENS, LAT + ROPE)
    blocks = TOKENS // TOK_DEV
    flat_ids = expert_ids.reshape(blocks, TOK_DEV * TOPK)
    onehot = (flat_ids[:, :, None] == jnp.arange(E, dtype=jnp.int32)[None, None, :]).astype(jnp.int32)
    slot_index = lax.optimization_barrier(jnp.sum(onehot * (jnp.cumsum(onehot, axis=1) - 1), axis=2)).astype(jnp.int32)
    destination = (jnp.arange(blocks, dtype=jnp.int32)[:, None] * CAP + slot_index).reshape(TOKENS, TOPK)
    token_index = jnp.broadcast_to(jnp.arange(TOKENS, dtype=jnp.int32)[:, None], (TOKENS, TOPK)).reshape(-1)
    padded = jnp.concatenate([normed_mid, jnp.zeros((1, D), dtype=jnp.bfloat16)], axis=0)

    def expert_step(routed_sum, expert):
        slot_target = jnp.where(expert_ids == expert, destination, blocks * CAP).reshape(-1)
        slot_token = jnp.full((blocks * CAP,), TOKENS, dtype=jnp.int32).at[slot_target].set(token_index, mode='drop')
        slot_gate = jnp.zeros((blocks * CAP,), dtype=jnp.float32).at[slot_target].set(gate_weights.reshape(-1), mode='drop')
        slot_rows = padded[slot_token]
        gate_full = jnp.concatenate([w_gate[2 * expert], w_gate[2 * expert + 1]], axis=1)
        up_full = jnp.concatenate([w_up[2 * expert], w_up[2 * expert + 1]], axis=1)
        down_full = jnp.concatenate([w_down[2 * expert], w_down[2 * expert + 1]], axis=0)
        gate_proj = jnp.dot(slot_rows, gate_full, preferred_element_type=jnp.float32)
        up_proj = jnp.dot(slot_rows, up_full, preferred_element_type=jnp.float32)
        activated = (jax.nn.silu(gate_proj) * up_proj).astype(jnp.bfloat16)
        expert_out = jnp.dot(activated, down_full, preferred_element_type=jnp.float32).astype(jnp.bfloat16)
        expert_out = lax.optimization_barrier(expert_out).astype(jnp.float32)
        routed_sum = routed_sum.at[slot_token].add(slot_gate[:, None] * expert_out, mode='drop')
        return (routed_sum, None)
    routed_sum, unused = lax.scan(expert_step, jnp.zeros((TOKENS, D), dtype=jnp.float32), jnp.arange(E, dtype=jnp.int32))
    hidden_out = (residual + routed_sum).astype(jnp.bfloat16)
    return (hidden_out, new_cache)
```

```python
import functools

import jax
import jax.numpy as jnp
import numpy as np
from jax import lax
from jax.experimental import pallas as pl
from jax.experimental.pallas import tpu as pltpu
from jax.sharding import Mesh
from jax.sharding import PartitionSpec as P

EPSILON = 1e-06
FLOOR_SCORE = -1e30
PARTS = 2
CHIP = ("req", "ylo")
BF16 = jnp.bfloat16
F32 = jnp.float32
NT = (((1,), (1,)), ((), ()))


def dot(a, b):
    return jnp.dot(a, b, preferred_element_type=F32)


def dot_nt(a, b):
    return lax.dot_general(a, b, NT, preferred_element_type=F32)


def iota(shape, axis):
    return lax.broadcasted_iota(jnp.int32, shape, axis)


def seg_starts(lengths_ref, pos):
    end_0 = lengths_ref[0, 0]
    end_1 = end_0 + lengths_ref[0, 1]
    return jnp.where(pos >= end_1, end_1, jnp.where(pos >= end_0, end_0, 0))


def route_kernel(depth, ids_ref, gates_ref, place_ref, mix_ref):
    top, rows = ids_ref.shape
    parts, part_slots, _ = place_ref.shape
    experts = part_slots // depth
    e_iota = iota((experts, rows), 0)
    named = jnp.zeros((experts, rows), F32)
    gate = jnp.zeros((experts, rows), F32)
    for k in range(top):
        hit = ids_ref[k : k + 1, :] == e_iota
        named = named + jnp.where(hit, 1.0, 0.0)
        gate = gate + jnp.where(hit, gates_ref[k : k + 1, :], 0.0)
    before = jnp.where(iota((rows, rows), 0) < iota((rows, rows), 1), 1.0, 0.0).astype(BF16)
    rank = dot(named.astype(BF16), before)
    order = (named * (rank + 1.0)).astype(BF16)
    gate_high = gate.astype(BF16)
    gate_low = (gate - gate_high.astype(F32)).astype(BF16)
    owner = iota((part_slots, experts), 0) // depth
    spread = jnp.where(owner == iota((part_slots, experts), 1), 1.0, 0.0).astype(BF16)
    order_at = dot(spread, order)
    high_at = dot(spread, gate_high)
    low_at = dot(spread, gate_low)
    level = (iota((part_slots, rows), 0) % depth).astype(F32)
    for part in range(parts):
        put = order_at == level + (1.0 + part * depth)
        place_ref[part] = jnp.where(put, 1.0, 0.0).astype(BF16)
        mix_ref[part, :rows] = jnp.where(put, high_at, 0.0).T.astype(BF16)
        mix_ref[part, rows:] = jnp.where(put, low_at, 0.0).T.astype(BF16)


def project_kernel(
    lengths_ref, sub_ref, tokens_ref, gain_ref, wq_ref, wl_ref, lgain_ref, wk_ref, inverse_ref,
    cache_ref, query_ref, normed, angle,
):
    rows = tokens_ref.shape[0]
    heads, nope, lat = wk_ref.shape
    rope = wl_ref.shape[0] - lat
    half = rope // 2

    @pl.when(pl.program_id(0) == 0)
    def _():
        x = tokens_ref[...].astype(F32)
        scale = lax.rsqrt(jnp.mean(x * x, axis=-1, keepdims=True) + EPSILON)
        normed[...] = (x * scale * gain_ref[...]).astype(BF16)
        pos = sub_ref[0] * rows + iota((half, rows), 1)
        offset = sub_ref[1] + pos - seg_starts(lengths_ref, pos)
        angles = offset.astype(F32) * inverse_ref[...]
        cos_part = jnp.cos(angles)
        sin_part = jnp.sin(angles)
        angle[...] = jnp.concatenate([cos_part, sin_part], axis=0).T
        latent = dot_nt(wl_ref[...], normed[...])
        low = latent[:lat]
        scale = lax.rsqrt(jnp.mean(low * low, axis=0, keepdims=True) + EPSILON)
        gain = jnp.broadcast_to(lgain_ref[...], (rows, lat)).T
        cache_ref[:lat] = (low * scale * gain).astype(BF16)
        first = latent[lat : lat + half]
        second = latent[lat + half :]
        cache_ref[lat : lat + half] = (first * cos_part - second * sin_part).astype(BF16)
        cache_ref[lat + half :] = (second * cos_part + first * sin_part).astype(BF16)

    queries = dot(normed[...], wq_ref[...]).astype(BF16)
    cos_part = angle[:, :half]
    sin_part = angle[:, half:]
    for h in range(heads):
        base = h * (nope + rope)
        query_ref[h, :, :lat] = dot(queries[:, base : base + nope], wk_ref[h]).astype(BF16)
        first = queries[:, base + nope : base + nope + half].astype(F32)
        second = queries[:, base + nope + half : base + nope + rope].astype(F32)
        query_ref[h, :, lat:] = jnp.concatenate(
            [first * cos_part - second * sin_part, second * cos_part + first * sin_part], axis=1
        ).astype(BF16)


def attend_kernel(
    score_scale, lengths_ref, sub_ref, query_ref, own_ref, back_1_ref, back_2_ref, back_3_ref, near_ref, far_ref,
    wv_ref, wo_ref, tokens_ref, gain_ref, place_ref,
    residual_ref, mid_ref, out_ref, keys, bias,
):
    rows = tokens_ref.shape[0]
    heads, _, width = query_ref.shape
    lat = wv_ref.shape[1]
    step = pl.program_id(0)
    tiles = near_ref.shape[0] + far_ref.shape[0]
    suffix = (own_ref, back_1_ref, back_2_ref, back_3_ref)

    @pl.when(step == 0)
    def _():
        for i in range(near_ref.shape[0]):
            keys[:, i * rows : (i + 1) * rows] = near_ref[i]
        for i in range(far_ref.shape[0]):
            at = (near_ref.shape[0] + i) * rows
            keys[:, at : at + rows] = far_ref[i]
        pos = sub_ref[0] * rows + iota((rows, rows), 0)
        start = seg_starts(lengths_ref, pos)
        for d, ref in enumerate(suffix):
            keys[:, (tiles + d) * rows : (tiles + d + 1) * rows] = ref[...]
            key_pos = ((sub_ref[0] + len(suffix) - d) % len(suffix)) * rows + iota((rows, rows), 1)
            allowed = (key_pos >= start) & (key_pos <= pos)
            bias[:, d * rows : (d + 1) * rows] = jnp.where(allowed, 0.0, FLOOR_SCORE)
        residual_ref[...] = tokens_ref[...].astype(F32)

    query = query_ref[...].reshape(heads * rows, width)
    scores = dot(query, keys[...]) * score_scale
    cut = tiles * rows
    mask = jnp.concatenate([bias[...]] * heads, axis=0)
    scores = jnp.concatenate([scores[:, :cut], scores[:, cut:] + mask], axis=1)
    weights = jnp.exp(scores - jnp.max(scores, axis=1, keepdims=True))
    denominator = jnp.sum(weights, axis=1, keepdims=True)
    latent_out = (dot_nt(weights.astype(BF16), keys[:lat]) / denominator).astype(BF16)
    head_out = jnp.concatenate(
        [dot(latent_out[h * rows : (h + 1) * rows], wv_ref[h]).astype(BF16) for h in range(heads)],
        axis=1,
    )
    residual_ref[...] += dot(head_out, wo_ref[...])

    @pl.when(step == pl.num_programs(0) - 1)
    def _():
        x = residual_ref[...]
        scale = lax.rsqrt(jnp.mean(x * x, axis=-1, keepdims=True) + EPSILON)
        mid = (x * scale * gain_ref[...]).astype(BF16)
        mid_ref[...] = mid
        out_ref[...] = dot(place_ref[...], mid).astype(BF16)


def place_kernel(place_ref, mid_ref, out_ref):
    out_ref[...] = dot(place_ref[...], mid_ref[...]).astype(BF16)


def expert_kernel(x_ref, g0, u0, d0, g1, u1, d1, out_ref, buf, sems):
    copies = [
        pltpu.make_async_copy(src, buf.at[i], sems.at[i])
        for i, src in enumerate((g0, u0, g1, u1, d0, d1))
    ]
    for copy in copies:
        copy.start()
    activated = []
    for half in range(2):
        copies[2 * half].wait()
        gate = dot_nt(x_ref[...], buf[2 * half])
        copies[2 * half + 1].wait()
        up = dot_nt(x_ref[...], buf[2 * half + 1])
        activated.append((gate / (1.0 + jnp.exp(-gate)) * up).astype(BF16))
    copies[4].wait()
    total = dot(activated[0], buf[4])
    copies[5].wait()
    out_ref[...] = (total + dot(activated[1], buf[5])).astype(BF16)


def mix_kernel(base_ref, mix_ref, rows_ref, out_ref):
    rows = base_ref.shape[0]
    both = dot(mix_ref[...], rows_ref[...])
    out_ref[...] = (base_ref[...] + (both[:rows] + both[rows:])).astype(out_ref.dtype)


def cost(flops, moved):
    return pl.CostEstimate(flops=int(flops), bytes_accessed=int(moved), transcendentals=0)


SMEM = pl.BlockSpec(memory_space=pltpu.SMEM)


def whole(array):
    return pl.BlockSpec(array.shape, lambda *_: (0,) * array.ndim)


def local(
    tokens, attn_gain, w_query, w_latent, latent_gain, w_key_up, w_value_up, w_out, moe_gain,
    w_gate, w_up, w_down, expert_ids, gate_weights, lengths, slab_group, owners, prefix_pool,
):
    rows, model = tokens.shape
    head_count, nope, lat = w_key_up.shape
    width = w_latent.shape[1]
    rope = width - lat
    value = w_value_up.shape[2]
    prefix_len = prefix_pool.shape[1]
    hidden = w_down.shape[1]
    top = expert_ids.shape[1]
    req_count = lax.axis_size("req")
    core_count = lax.axis_size("core")
    sub_count = lax.axis_size("ylo") * core_count
    chips = req_count * lax.axis_size("ylo")
    sub = lax.axis_index("ylo") * core_count + lax.axis_index("core")
    place_info = jnp.stack([sub, jnp.int32(prefix_len)]).astype(jnp.int32)

    quarter_len = prefix_len // sub_count
    quarter = lax.dynamic_slice(prefix_pool[0].T, (0, sub * quarter_len), (width, quarter_len))
    lanes = 128
    piece = width * quarter_len // lanes // req_count
    pieces = (
        quarter.reshape(width, quarter_len // lanes, lanes).transpose(1, 0, 2)
        .reshape(req_count, piece, lanes)
    )
    tag_rows = -piece % 8 or 8
    tag = jnp.broadcast_to(slab_group[0].astype(BF16), (req_count, tag_rows, lanes))
    spread = lax.all_to_all(
        jnp.concatenate([pieces, tag], axis=1), "req", split_axis=0, concat_axis=0, tiled=True
    )
    groups = spread[:, piece, 0].astype(jnp.int32)
    slots = jnp.sum(
        jnp.where(
            groups[:, None] == jnp.arange(owners.shape[0], dtype=jnp.int32)[None, :], owners[None, :], 0
        ),
        axis=1,
    )
    picked = jnp.take(spread, slots, axis=0, mode="clip")
    ylo_count = lax.axis_size("ylo")
    doubled = jnp.broadcast_to(picked[:, None], (req_count, ylo_count) + picked.shape[1:])
    near = lax.all_to_all(
        doubled.reshape((chips,) + picked.shape[1:]), CHIP, split_axis=0, concat_axis=0, tiled=True
    )
    near = near[:, :piece].reshape(req_count, ylo_count, piece, lanes).transpose(1, 0, 2, 3)
    near = near.reshape(ylo_count * quarter_len // lanes, width, lanes)
    swap = [(0, 1), (1, 0)]
    far = lax.ppermute(near, "core", swap)

    gate_t = w_gate[0].T
    up_t = w_up[0].T
    down = w_down[0]
    gate_far = lax.ppermute(gate_t, "core", swap)
    up_far = lax.ppermute(up_t, "core", swap)
    down_far = lax.ppermute(down, "core", swap)

    pair = 2
    steps = head_count // pair
    inverse = (10000.0 ** (-np.arange(rope // 2) / (rope // 2))).astype(np.float32)
    inverse = jnp.broadcast_to(jnp.asarray(inverse)[:, None], (rope // 2, rows))
    w_latent_t = w_latent.T
    gain_row = attn_gain[None, :]
    lgain_row = latent_gain[None, :]
    cache_t, query_full = pl.pallas_call(
        project_kernel,
        name="project",
        grid=(steps,),
        in_specs=[
            SMEM, SMEM, whole(tokens), whole(gain_row),
            pl.BlockSpec((model, pair * (nope + rope)), lambda i: (0, i)),
            whole(w_latent_t), whole(lgain_row),
            pl.BlockSpec((pair, nope, lat), lambda i: (i, 0, 0)),
            whole(inverse),
        ],
        out_specs=[
            pl.BlockSpec((width, rows), lambda i: (0, 0)),
            pl.BlockSpec((pair, rows, width), lambda i: (i, 0, 0)),
        ],
        out_shape=[
            jax.ShapeDtypeStruct((width, rows), BF16),
            jax.ShapeDtypeStruct((head_count, rows, width), BF16),
        ],
        scratch_shapes=[pltpu.VMEM((rows, model), BF16), pltpu.VMEM((rows, rope), F32)],
        cost_estimate=cost(2 * rows * model * (w_query.shape[1] + width), 14e6),
    )(lengths, place_info, tokens, gain_row, w_query, w_latent_t, lgain_row, w_key_up, inverse)

    back = [
        lax.ppermute(cache_t, ("ylo", "core"), [(k, (k + d) % sub_count) for k in range(sub_count)])
        for d in range(1, sub_count)
    ]

    slot_count = 4 * rows * top // 3
    part_slots = slot_count // PARTS
    depth = part_slots // chips
    ids_t = expert_ids.T
    gates_t = gate_weights.T
    placing, mixing = pl.pallas_call(
        functools.partial(route_kernel, depth),
        name="route",
        in_specs=[whole(ids_t), whole(gates_t)],
        out_specs=[
            pl.BlockSpec((PARTS, part_slots, rows), lambda: (0, 0, 0)),
            pl.BlockSpec((PARTS, 2 * rows, part_slots), lambda: (0, 0, 0)),
        ],
        out_shape=[
            jax.ShapeDtypeStruct((PARTS, part_slots, rows), BF16),
            jax.ShapeDtypeStruct((PARTS, 2 * rows, part_slots), BF16),
        ],
        cost_estimate=cost(1e9, 2e6),
    )(ids_t, gates_t)

    moe_row = moe_gain[None, :]
    residual, mid, first_out = pl.pallas_call(
        functools.partial(attend_kernel, (nope + rope) ** (-0.5)),
        name="attend",
        grid=(steps,),
        in_specs=[
            SMEM, SMEM,
            pl.BlockSpec((pair, rows, width), lambda i: (i, 0, 0)),
            whole(cache_t), whole(cache_t), whole(cache_t), whole(cache_t), whole(near), whole(far),
            pl.BlockSpec((pair, lat, value), lambda i: (i, 0, 0)),
            pl.BlockSpec((pair * value, model), lambda i: (i, 0)),
            whole(tokens), whole(moe_row),
            pl.BlockSpec((None, part_slots, rows), lambda i: (0, 0, 0)),
        ],
        out_specs=[
            pl.BlockSpec((rows, model), lambda i: (0, 0)),
            pl.BlockSpec((rows, model), lambda i: (0, 0)),
            pl.BlockSpec((part_slots, model), lambda i: (0, 0)),
        ],
        out_shape=[
            jax.ShapeDtypeStruct((rows, model), F32),
            jax.ShapeDtypeStruct((rows, model), BF16),
            jax.ShapeDtypeStruct((part_slots, model), BF16),
        ],
        scratch_shapes=[
            pltpu.VMEM((width, prefix_len + rows * sub_count), BF16),
            pltpu.VMEM((rows, rows * sub_count), F32),
        ],
        cost_estimate=cost(8e9, 14e6),
    )(
        lengths, place_info, query_full, cache_t, *back, near, far,
        w_value_up, w_out, tokens, moe_row, placing,
    )

    def exchange(x):
        x = x.reshape(chips, depth, model)
        return lax.all_to_all(x, CHIP, split_axis=0, concat_axis=0, tiled=True).reshape(part_slots, model)

    def place(part):
        return pl.pallas_call(
            place_kernel,
            name="place",
            grid=(2,),
            in_specs=[
                pl.BlockSpec((None, part_slots // 2, rows), lambda i: (part, i, 0)), whole(mid),
            ],
            out_specs=pl.BlockSpec((part_slots // 2, model), lambda i: (i, 0)),
            out_shape=jax.ShapeDtypeStruct((part_slots, model), BF16),
            cost_estimate=cost(2 * part_slots * rows * model, 3e6),
        )(placing, mid)

    any_spec = pl.BlockSpec(memory_space=pl.ANY)

    def experts(x):
        return pl.pallas_call(
            expert_kernel,
            name="experts",
            in_specs=[whole(x)] + [any_spec] * 6,
            out_specs=pl.BlockSpec((part_slots, model), lambda: (0, 0)),
            out_shape=jax.ShapeDtypeStruct((part_slots, model), BF16),
            scratch_shapes=[
                pltpu.VMEM((6, hidden, model), BF16), pltpu.SemaphoreType.DMA((6,)),
            ],
            cost_estimate=cost(12 * part_slots * model * hidden, 21e6),
        )(x, gate_t, up_t, down, gate_far, up_far, down_far)

    blocks = 4

    def mix(base, part, x, dtype):
        return pl.pallas_call(
            mix_kernel,
            name="mix",
            grid=(blocks,),
            in_specs=[
                pl.BlockSpec((rows, model // blocks), lambda i: (0, i)),
                pl.BlockSpec((None, 2 * rows, part_slots), lambda i: (part, 0, 0)),
                pl.BlockSpec((part_slots, model // blocks), lambda i: (0, i)),
            ],
            out_specs=pl.BlockSpec((rows, model // blocks), lambda i: (0, i)),
            out_shape=jax.ShapeDtypeStruct((rows, model), dtype),
            cost_estimate=cost(4 * part_slots * rows * model, 5e6),
        )(base, mixing, x)

    outbound = [first_out] + [place(part) for part in range(1, PARTS)]
    arrived = [exchange(x) for x in outbound]
    returned = [exchange(experts(x)) for x in arrived]
    total = residual
    for part in range(PARTS):
        total = mix(total, part, returned[part], BF16 if part == PARTS - 1 else F32)
    return (total, cache_t.T)


def solution(mesh):
    split = Mesh(mesh.devices.reshape(mesh.devices.shape[0], -1, 2), ("req", "ylo", "core"))
    every = ("req", "ylo", "core")
    in_specs = (
        P(every, None), P(), P(), P(), P(), P(), P(), P(), P(),
        P(every, None, None), P(every, None, None), P(every, None, None),
        P(every, None), P(every, None), P("req", None), P("req"), P(), P("req", None, None),
    )
    out_specs = (P(every, None), P(every, None))
    return jax.shard_map(local, mesh=split, in_specs=in_specs, out_specs=out_specs, check_vma=False)
```

```python
import functools
import math

import jax
import jax.numpy as jnp
import numpy as np
from jax import lax
from jax.experimental import pallas as pl
from jax.experimental.pallas import tpu as pltpu
from jax.sharding import Mesh
from jax.sharding import PartitionSpec as P


EPSILON = 1e-06
FLOOR_SCORE = -1e30
PARTS = 2
CHIP = ("req", "ylo")
BF16 = jnp.bfloat16
F32 = jnp.float32
NT = (((1,), (1,)), ((), ()))


def dot(a, b):
    return jnp.dot(a, b, preferred_element_type=F32)


def dot_nt(a, b):
    return lax.dot_general(a, b, NT, preferred_element_type=F32)


def iota(shape, axis):
    return lax.broadcasted_iota(jnp.int32, shape, axis)


def seg_starts(lengths_ref, pos):
    end_0 = lengths_ref[0, 0]
    end_1 = end_0 + lengths_ref[0, 1]
    return jnp.where(pos >= end_1, end_1, jnp.where(pos >= end_0, end_0, 0))


def spread_matrix(part_slots, experts):
    owner = iota((part_slots, experts), 0) // (part_slots // experts)
    return jnp.where(owner == iota((part_slots, experts), 1), 1.0, 0.0).astype(BF16)


def route_kernel(depth, ids_ref, place_ref):
    top, rows = ids_ref.shape
    parts, part_slots, _ = place_ref.shape
    experts = part_slots // depth
    e_iota = iota((experts, rows), 0)
    named = jnp.zeros((experts, rows), F32)
    for k in range(top):
        named = named + jnp.where(ids_ref[k : k + 1, :] == e_iota, 1.0, 0.0)
    before = jnp.where(iota((rows, rows), 0) < iota((rows, rows), 1), 1.0, 0.0).astype(BF16)
    rank = dot(named.astype(BF16), before)
    order = (named * (rank + 1.0)).astype(BF16)
    order_at = dot(spread_matrix(part_slots, experts), order)
    level = (iota((part_slots, rows), 0) % depth).astype(F32)
    for part in range(parts):
        put = order_at == level + (1.0 + part * depth)
        place_ref[part] = jnp.where(put, 1.0, 0.0).astype(BF16)


def gate_kernel(depth, part, ids_ref, gates_ref, place_ref, mix_ref):
    top, rows = ids_ref.shape
    part_slots = place_ref.shape[1]
    experts = part_slots // depth
    e_iota = iota((experts, rows), 0)
    gate = jnp.zeros((experts, rows), F32)
    for k in range(top):
        gate = gate + jnp.where(ids_ref[k : k + 1, :] == e_iota, gates_ref[k : k + 1, :], 0.0)
    gate_high = gate.astype(BF16)
    gate_low = (gate - gate_high.astype(F32)).astype(BF16)
    spread = spread_matrix(part_slots, experts)
    put = place_ref[part].astype(F32) > 0.5
    mix_ref[:rows] = jnp.where(put, dot(spread, gate_high), 0.0).T.astype(BF16)
    mix_ref[rows:] = jnp.where(put, dot(spread, gate_low), 0.0).T.astype(BF16)


def project_kernel(
    lengths_ref, sub_ref, tokens_ref, gain_ref, wq_ref, wl_ref, lgain_ref, wk_ref, inverse_ref,
    cache_ref, query_ref, normed, angle,
):
    rows = tokens_ref.shape[0]
    heads, nope, lat = wk_ref.shape
    rope = wl_ref.shape[0] - lat
    half = rope // 2

    @pl.when(pl.program_id(0) == 0)
    def _():
        x = tokens_ref[...].astype(F32)
        scale = lax.rsqrt(jnp.mean(x * x, axis=-1, keepdims=True) + EPSILON)
        normed[...] = (x * scale * gain_ref[...]).astype(BF16)
        pos = sub_ref[0] * rows + iota((half, rows), 1)
        offset = sub_ref[1] + pos - seg_starts(lengths_ref, pos)
        angles = offset.astype(F32) * inverse_ref[...]
        cos_part = jnp.cos(angles)
        sin_part = jnp.sin(angles)
        angle[...] = jnp.concatenate([cos_part, sin_part], axis=0).T
        latent = dot_nt(wl_ref[...], normed[...])
        low = latent[:lat]
        scale = lax.rsqrt(jnp.mean(low * low, axis=0, keepdims=True) + EPSILON)
        gain = jnp.broadcast_to(lgain_ref[...], (rows, lat)).T
        cache_ref[:lat] = (low * scale * gain).astype(BF16)
        first = latent[lat : lat + half]
        second = latent[lat + half :]
        cache_ref[lat : lat + half] = (first * cos_part - second * sin_part).astype(BF16)
        cache_ref[lat + half :] = (second * cos_part + first * sin_part).astype(BF16)

    queries = dot(normed[...], wq_ref[...]).astype(BF16)
    cos_part = angle[:, :half]
    sin_part = angle[:, half:]
    for h in range(heads):
        base = h * (nope + rope)
        at = pl.program_id(0) * heads + h
        query_ref[at, :, :lat] = dot(queries[:, base : base + nope], wk_ref[h]).astype(BF16)
        first = queries[:, base + nope : base + nope + half].astype(F32)
        second = queries[:, base + nope + half : base + nope + rope].astype(F32)
        query_ref[at, :, lat:] = jnp.concatenate(
            [first * cos_part - second * sin_part, second * cos_part + first * sin_part], axis=1
        ).astype(BF16)


def attend_kernel(
    score_scale, lengths_ref, sub_ref, query_ref, own_ref, back_1_ref, back_2_ref, back_3_ref,
    near_ref, far_ref, gain_ref, wv_hbm, wo_hbm, tokens_hbm, place_hbm,
    residual_ref, mid_ref, out_ref,
    keys, bias, query_buf, wv_ref, wo_ref, tokens_ref, place_ref, sems,
):
    copies = [
        pltpu.make_async_copy(src, dst, sems.at[i])
        for i, (src, dst) in enumerate((
            (query_ref, query_buf), (wv_hbm, wv_ref), (wo_hbm, wo_ref), (tokens_hbm, tokens_ref),
            (place_hbm.at[0], place_ref),
        ))
    ]
    for copy in copies:
        copy.start()
    rows = tokens_ref.shape[0]
    heads, lat, _ = wv_ref.shape
    width = query_ref.shape[2]
    near_tiles = near_ref.shape[0]
    tiles = near_tiles + far_ref.shape[0]
    suffix = (own_ref, back_1_ref, back_2_ref, back_3_ref)
    for i in range(near_tiles):
        keys[:, i * rows : (i + 1) * rows] = near_ref[i]
        keys[:, (near_tiles + i) * rows : (near_tiles + i + 1) * rows] = far_ref[i]
    pos = sub_ref[0] * rows + iota((rows, rows), 0)
    start = seg_starts(lengths_ref, pos)
    for d, ref in enumerate(suffix):
        keys[:, (tiles + d) * rows : (tiles + d + 1) * rows] = ref[...]
        key_pos = ((sub_ref[0] + len(suffix) - d) % len(suffix)) * rows + iota((rows, rows), 1)
        allowed = (key_pos >= start) & (key_pos <= pos)
        bias[:, d * rows : (d + 1) * rows] = jnp.where(allowed, 0.0, FLOOR_SCORE)
    cut = tiles * rows
    pair = 2
    mask = jnp.concatenate([bias[...]] * pair, axis=0)

    def score(i):
        query = query_buf[i * pair : (i + 1) * pair].reshape(pair * rows, width)
        return dot(query, keys[:, :cut]), dot(query, keys[:, cut:]) + mask

    def attend(early, late):
        row_top = jnp.maximum(
            jnp.max(early, axis=1, keepdims=True), jnp.max(late, axis=1, keepdims=True)
        )
        early = jnp.exp2((early - row_top) * score_scale)
        late = jnp.exp2((late - row_top) * score_scale)
        denominator = jnp.sum(early, axis=1, keepdims=True) + jnp.sum(late, axis=1, keepdims=True)
        weighted = dot_nt(early.astype(BF16), keys[:lat, :cut]) + dot_nt(
            late.astype(BF16), keys[:lat, cut:]
        )
        return (weighted / denominator).astype(BF16)

    latent_out = []
    copies[0].wait()
    current = score(0)
    for i in range(heads // pair):
        following = score(i + 1) if i + 1 < heads // pair else None
        latent_out.append(attend(*current))
        current = following
    copies[1].wait()
    head_out = jnp.concatenate(
        [
            dot(latent_out[h // pair][h % pair * rows : (h % pair + 1) * rows], wv_ref[h]).astype(BF16)
            for h in range(heads)
        ],
        axis=1,
    )
    copies[2].wait()
    copies[3].wait()
    x = tokens_ref[...].astype(F32) + dot(head_out, wo_ref[...])
    residual_ref[...] = x
    scale = lax.rsqrt(jnp.mean(x * x, axis=-1, keepdims=True) + EPSILON)
    mid = (x * scale * gain_ref[...]).astype(BF16)
    mid_ref[...] = mid
    copies[4].wait()
    out_ref[...] = dot(place_ref[...], mid).astype(BF16)


def place_kernel(place_ref, mid_ref, out_ref):
    out_ref[...] = dot(place_ref[...], mid_ref[...]).astype(BF16)


def expert_kernel(x_ref, g0, u0, d0, g1, u1, d1, out_ref, buf, activated, sems):
    copies = [
        pltpu.make_async_copy(src, buf.at[i], sems.at[i])
        for i, src in enumerate((g0, u0, g1, u1, d0, d1))
    ]
    for copy in copies:
        copy.start()
    step = 256
    blocks = x_ref.shape[0] // step
    for half in range(2):
        copies[2 * half].wait()
        copies[2 * half + 1].wait()

        @pl.loop(0, blocks)
        def _(i):
            at = pl.ds(pl.multiple_of(i * step, step), step)
            gate = dot_nt(x_ref[at], buf[2 * half])
            up = dot_nt(x_ref[at], buf[2 * half + 1])
            activated[half, at] = (gate / (1.0 + jnp.exp(-gate)) * up).astype(BF16)

    copies[4].wait()
    copies[5].wait()

    @pl.loop(0, blocks)
    def _(i):
        at = pl.ds(pl.multiple_of(i * step, step), step)
        total = dot(activated[0, at], buf[4])
        out_ref[at] = (total + dot(activated[1, at], buf[5])).astype(BF16)


def mix_kernel(base_ref, mix_ref, rows_ref, out_ref):
    rows = base_ref.shape[0]
    both = dot(mix_ref[...], rows_ref[...])
    out_ref[...] = (base_ref[...] + (both[:rows] + both[rows:])).astype(out_ref.dtype)


def cost(flops, moved):
    return pl.CostEstimate(flops=int(flops), bytes_accessed=int(moved), transcendentals=0)


SMEM = pl.BlockSpec(memory_space=pltpu.SMEM)
VMEM = pl.BlockSpec(memory_space=pltpu.VMEM)
HBM = pl.BlockSpec(memory_space=pltpu.HBM)


def near_core(x):
    return pltpu.with_memory_space_constraint(x, pltpu.VMEM)


def limit(mebibytes):
    return pltpu.CompilerParams(vmem_limit_bytes=mebibytes << 20)


def whole(array):
    return pl.BlockSpec(array.shape, lambda *_: (0,) * array.ndim)


def layer(
    tokens, attn_gain, w_query, w_latent, latent_gain, w_key_up, w_value_up, w_out, moe_gain,
    w_gate, w_up, w_down, expert_ids, gate_weights, lengths, slab_group, owners, prefix_pool,
):
    rows, model = tokens.shape
    head_count, nope, lat = w_key_up.shape
    width = w_latent.shape[1]
    rope = width - lat
    prefix_len = prefix_pool.shape[1]
    hidden = w_down.shape[1]
    top = expert_ids.shape[1]
    req_count = lax.axis_size("req")
    core_count = lax.axis_size("core")
    sub_count = lax.axis_size("ylo") * core_count
    chips = req_count * lax.axis_size("ylo")
    sub = lax.axis_index("ylo") * core_count + lax.axis_index("core")
    place_info = jnp.stack([sub, jnp.int32(prefix_len)]).astype(jnp.int32)

    quarter_len = prefix_len // sub_count
    quarter = lax.dynamic_slice(prefix_pool[0].T, (0, sub * quarter_len), (width, quarter_len))
    lanes = 128
    piece = width * quarter_len // lanes // req_count
    pieces = (
        quarter.reshape(width, quarter_len // lanes, lanes).transpose(1, 0, 2)
        .reshape(req_count, piece, lanes)
    )
    tag_rows = -piece % 8 or 8
    tag = jnp.broadcast_to(slab_group[0].astype(BF16), (req_count, tag_rows, lanes))
    spread = lax.all_to_all(
        jnp.concatenate([pieces, tag], axis=1), "req", split_axis=0, concat_axis=0, tiled=True
    )
    groups = spread[:, piece, 0].astype(jnp.int32)
    slots = jnp.sum(
        jnp.where(
            groups[:, None] == jnp.arange(owners.shape[0], dtype=jnp.int32)[None, :], owners[None, :], 0
        ),
        axis=1,
    )
    picked = jnp.take(spread, slots, axis=0, mode="clip")
    ylo_count = lax.axis_size("ylo")
    doubled = jnp.broadcast_to(picked[:, None], (req_count, ylo_count) + picked.shape[1:])
    near = lax.all_to_all(
        doubled.reshape((chips,) + picked.shape[1:]), CHIP, split_axis=0, concat_axis=0, tiled=True
    )
    near = near[:, :piece].reshape(req_count, ylo_count, piece, lanes).transpose(1, 0, 2, 3)
    near = near.reshape(ylo_count * quarter_len // lanes, width, lanes)
    swap = [(0, 1), (1, 0)]
    far = lax.ppermute(near, "core", swap)

    gate_t = w_gate[0].T
    up_t = w_up[0].T
    down = w_down[0]
    gate_far = lax.ppermute(gate_t, "core", swap)
    up_far = lax.ppermute(up_t, "core", swap)
    down_far = lax.ppermute(down, "core", swap)

    pair = 2
    steps = head_count // pair
    inverse = (10000.0 ** (-np.arange(rope // 2) / (rope // 2))).astype(np.float32)
    inverse = jnp.broadcast_to(jnp.asarray(inverse)[:, None], (rope // 2, rows))
    w_latent_t = w_latent.T
    gain_row = attn_gain[None, :]
    lgain_row = latent_gain[None, :]
    cache_t, query_full = pl.pallas_call(
        project_kernel,
        name="project",
        grid=(steps,),
        in_specs=[
            SMEM, SMEM, whole(tokens), whole(gain_row),
            pl.BlockSpec((model, pair * (nope + rope)), lambda i: (0, i)),
            whole(w_latent_t), whole(lgain_row),
            pl.BlockSpec((pair, nope, lat), lambda i: (i, 0, 0)),
            whole(inverse),
        ],
        out_specs=[VMEM, VMEM],
        out_shape=[
            pltpu.HBM((width, rows), BF16),
            pltpu.HBM((head_count, rows, width), BF16),
        ],
        scratch_shapes=[pltpu.VMEM((rows, model), BF16), pltpu.VMEM((rows, rope), F32)],
        cost_estimate=cost(2 * rows * model * (w_query.shape[1] + width), 14e6),
    )(lengths, place_info, tokens, gain_row, w_query, w_latent_t, lgain_row, w_key_up, inverse)

    back = [
        lax.ppermute(cache_t, ("ylo", "core"), [(k, (k + d) % sub_count) for k in range(sub_count)])
        for d in range(1, sub_count)
    ]

    slot_count = 4 * rows * top // 3
    part_slots = slot_count // PARTS
    depth = part_slots // chips
    ids_t = expert_ids.T
    gates_t = gate_weights.T
    placing = pl.pallas_call(
        functools.partial(route_kernel, depth),
        name="route",
        in_specs=[whole(ids_t)],
        out_specs=VMEM,
        out_shape=pltpu.HBM((PARTS, part_slots, rows), BF16),
        cost_estimate=cost(1e9, 2e6),
    )(ids_t)
    mixing = []
    for part in range(PARTS):
        mixing.append(pl.pallas_call(
            functools.partial(gate_kernel, depth, part),
            name="gates",
            in_specs=[whole(ids_t), whole(gates_t), VMEM],
            out_specs=VMEM,
            out_shape=pltpu.HBM((2 * rows, part_slots), BF16),
            cost_estimate=cost(1e9, 2e6),
        )(ids_t, gates_t, placing))

    moe_row = moe_gain[None, :]
    residual, mid, first_out = pl.pallas_call(
        functools.partial(attend_kernel, (nope + rope) ** (-0.5) * math.log2(math.e)),
        name="attend",
        in_specs=[SMEM, SMEM, HBM] + [VMEM] * 7 + [HBM] * 4,
        out_specs=[VMEM, VMEM, VMEM],
        out_shape=[
            pltpu.HBM((rows, model), F32),
            pltpu.HBM((rows, model), BF16),
            pltpu.HBM((part_slots, model), BF16),
        ],
        scratch_shapes=[
            pltpu.VMEM((width, prefix_len + rows * sub_count), BF16),
            pltpu.VMEM((rows, rows * sub_count), F32),
            pltpu.VMEM(query_full.shape, BF16),
            pltpu.VMEM(w_value_up.shape, BF16),
            pltpu.VMEM(w_out.shape, BF16),
            pltpu.VMEM(tokens.shape, BF16),
            pltpu.VMEM((part_slots, rows), BF16),
            pltpu.SemaphoreType.DMA((5,)),
        ],
        compiler_params=limit(54),
        cost_estimate=cost(5e9, 6e6),
    )(
        lengths, place_info, query_full, cache_t, *map(near_core, (*back, near, far)),
        moe_row, w_value_up, w_out, tokens, placing,
    )

    def exchange(x):
        x = x.reshape(chips, depth, model)
        x = lax.all_to_all(x, CHIP, split_axis=0, concat_axis=0, tiled=True)
        return x.reshape(part_slots, model)

    def place(part):
        return pl.pallas_call(
            place_kernel,
            name="place",
            grid=(2,),
            in_specs=[
                pl.BlockSpec((None, part_slots // 2, rows), lambda i: (part, i, 0)), VMEM,
            ],
            out_specs=pl.BlockSpec((part_slots // 2, model), lambda i: (i, 0)),
            out_shape=pltpu.HBM((part_slots, model), BF16),
            cost_estimate=cost(2 * part_slots * rows * model, 3e6),
        )(placing, mid)

    def experts(x):
        return pl.pallas_call(
            expert_kernel,
            name="experts",
            in_specs=[VMEM] + [HBM] * 6,
            out_specs=pl.BlockSpec((part_slots, model), lambda: (0, 0)),
            out_shape=pltpu.HBM((part_slots, model), BF16),
            scratch_shapes=[
                pltpu.VMEM((6, hidden, model), BF16), pltpu.VMEM((2, part_slots, hidden), BF16),
                pltpu.SemaphoreType.DMA((6,)),
            ],
            compiler_params=limit(54),
            cost_estimate=cost(12 * part_slots * model * hidden, 21e6),
        )(near_core(x), gate_t, up_t, down, gate_far, up_far, down_far)

    def mix(base, part, x, last):
        shape = (rows, model)
        return pl.pallas_call(
            mix_kernel,
            name="mix",
            in_specs=[VMEM] * 3,
            out_specs=VMEM,
            out_shape=pltpu.HBM(shape, BF16 if last else F32),
            compiler_params=limit(54),
            cost_estimate=cost(4 * part_slots * rows * model, 3e6),
        )(base, mixing[part], near_core(x))

    outbound = [first_out] + [place(part) for part in range(1, PARTS)]
    arrived = [exchange(x) for x in outbound]
    returned = [exchange(experts(x)) for x in arrived]
    total = residual
    for part in range(PARTS):
        total = mix(total, part, returned[part], part == PARTS - 1)
    return (total, cache_t.T)


def solution(mesh):
    split = Mesh(mesh.devices.reshape(mesh.devices.shape[0], -1, 2), ("req", "ylo", "core"))
    every = ("req", "ylo", "core")
    in_specs = (
        P(every, None), P(), P(), P(), P(), P(), P(), P(), P(),
        P(every, None, None), P(every, None, None), P(every, None, None),
        P(every, None), P(every, None), P("req", None), P("req"), P(), P("req", None, None),
    )
    out_specs = (P(every, None), P(every, None))
    return jax.shard_map(layer, mesh=split, in_specs=in_specs, out_specs=out_specs, check_vma=False)
```

```python
import functools
import math

import jax
import jax.numpy as jnp
import numpy as np
from jax import lax
from jax.experimental import pallas as pl
from jax.experimental.pallas import tpu as pltpu
from jax.sharding import Mesh
from jax.sharding import PartitionSpec as P


EPSILON = 1e-06
FLOOR_SCORE = -1e30
PARTS = 2
CHIP = ("req", "ylo")
BF16 = jnp.bfloat16
F32 = jnp.float32
NT = (((1,), (1,)), ((), ()))


def dot(a, b):
    return jnp.dot(a, b, preferred_element_type=F32)


def dot_nt(a, b):
    return lax.dot_general(a, b, NT, preferred_element_type=F32)


def iota(shape, axis):
    return lax.broadcasted_iota(jnp.int32, shape, axis)


def seg_starts(lengths_ref, pos):
    end_0 = lengths_ref[0, 0]
    end_1 = end_0 + lengths_ref[0, 1]
    return jnp.where(pos >= end_1, end_1, jnp.where(pos >= end_0, end_0, 0))


def spread_matrix(part_slots, experts):
    owner = iota((part_slots, experts), 0) // (part_slots // experts)
    return jnp.where(owner == iota((part_slots, experts), 1), 1.0, 0.0).astype(BF16)


def route_kernel(depth, ids_ref, place_ref):
    top, rows = ids_ref.shape
    parts, part_slots, _ = place_ref.shape
    experts = part_slots // depth
    e_iota = iota((experts, rows), 0)
    named = jnp.zeros((experts, rows), F32)
    for k in range(top):
        named = named + jnp.where(ids_ref[k : k + 1, :] == e_iota, 1.0, 0.0)
    before = jnp.where(iota((rows, rows), 0) < iota((rows, rows), 1), 1.0, 0.0).astype(BF16)
    rank = dot(named.astype(BF16), before)
    order = (named * (rank + 1.0)).astype(BF16)
    order_at = dot(spread_matrix(part_slots, experts), order)
    level = (iota((part_slots, rows), 0) % depth).astype(F32)
    for part in range(parts):
        put = order_at == level + (1.0 + part * depth)
        place_ref[part] = jnp.where(put, 1.0, 0.0).astype(BF16)


def gate_kernel(depth, part, ids_ref, gates_ref, place_ref, mix_ref):
    top, rows = ids_ref.shape
    part_slots = place_ref.shape[1]
    experts = part_slots // depth
    e_iota = iota((experts, rows), 0)
    gate = jnp.zeros((experts, rows), F32)
    for k in range(top):
        gate = gate + jnp.where(ids_ref[k : k + 1, :] == e_iota, gates_ref[k : k + 1, :], 0.0)
    gate_high = gate.astype(BF16)
    gate_low = (gate - gate_high.astype(F32)).astype(BF16)
    spread = spread_matrix(part_slots, experts)
    put = place_ref[part].astype(F32) > 0.5
    mix_ref[:rows] = jnp.where(put, dot(spread, gate_high), 0.0).T.astype(BF16)
    mix_ref[rows:] = jnp.where(put, dot(spread, gate_low), 0.0).T.astype(BF16)


def cache_kernel(
    lengths_ref, sub_ref, tokens_ref, gain_ref, wl_ref, lgain_ref, inverse_ref,
    cache_ref, normed_ref, angle_ref,
):
    rows = tokens_ref.shape[0]
    lat = lgain_ref.shape[1]
    half = (wl_ref.shape[0] - lat) // 2
    x = tokens_ref[...].astype(F32)
    scale = lax.rsqrt(jnp.mean(x * x, axis=-1, keepdims=True) + EPSILON)
    normed = (x * scale * gain_ref[...]).astype(BF16)
    normed_ref[...] = normed
    pos = sub_ref[0] * rows + iota((half, rows), 1)
    offset = sub_ref[1] + pos - seg_starts(lengths_ref, pos)
    angles = offset.astype(F32) * inverse_ref[...]
    cos_part = jnp.cos(angles)
    sin_part = jnp.sin(angles)
    angle_ref[...] = jnp.concatenate([cos_part, sin_part], axis=0).T
    latent = dot_nt(wl_ref[...], normed)
    low = latent[:lat]
    scale = lax.rsqrt(jnp.mean(low * low, axis=0, keepdims=True) + EPSILON)
    gain = jnp.broadcast_to(lgain_ref[...], (rows, lat)).T
    cache_ref[:lat] = (low * scale * gain).astype(BF16)
    first = latent[lat : lat + half]
    second = latent[lat + half :]
    cache_ref[lat : lat + half] = (first * cos_part - second * sin_part).astype(BF16)
    cache_ref[lat + half :] = (second * cos_part + first * sin_part).astype(BF16)


def query_kernel(normed_ref, angle_ref, wq_ref, wk_ref, query_ref):
    heads, nope, lat = wk_ref.shape
    rope = angle_ref.shape[1]
    half = rope // 2
    queries = dot(normed_ref[...], wq_ref[...]).astype(BF16)
    cos_part = angle_ref[:, :half]
    sin_part = angle_ref[:, half:]
    for h in range(heads):
        base = h * (nope + rope)
        query_ref[h, :, :lat] = dot(queries[:, base : base + nope], wk_ref[h]).astype(BF16)
        first = queries[:, base + nope : base + nope + half].astype(F32)
        second = queries[:, base + nope + half : base + nope + rope].astype(F32)
        query_ref[h, :, lat:] = jnp.concatenate(
            [first * cos_part - second * sin_part, second * cos_part + first * sin_part], axis=1
        ).astype(BF16)


def attend_kernel(
    score_scale, lengths_ref, sub_ref, query_ref, own_ref, back_1_ref, back_2_ref, back_3_ref,
    near_ref, far_ref, gain_ref, wv_hbm, wo_hbm, tokens_hbm, place_hbm,
    residual_ref, mid_ref, out_ref,
    keys, bias, query_buf, wv_ref, wo_ref, tokens_ref, place_ref, sems,
):
    copies = [
        pltpu.make_async_copy(src, dst, sems.at[i])
        for i, (src, dst) in enumerate((
            (query_ref, query_buf), (wv_hbm, wv_ref), (wo_hbm, wo_ref), (tokens_hbm, tokens_ref),
            (place_hbm.at[0], place_ref),
        ))
    ]
    for copy in copies:
        copy.start()
    rows = tokens_ref.shape[0]
    heads, lat, _ = wv_ref.shape
    width = query_ref.shape[2]
    near_tiles = near_ref.shape[0]
    tiles = near_tiles + far_ref.shape[0]
    suffix = (own_ref, back_1_ref, back_2_ref, back_3_ref)
    for i in range(near_tiles):
        keys[:, i * rows : (i + 1) * rows] = near_ref[i]
        keys[:, (near_tiles + i) * rows : (near_tiles + i + 1) * rows] = far_ref[i]
    pos = sub_ref[0] * rows + iota((rows, rows), 0)
    start = seg_starts(lengths_ref, pos)
    for d, ref in enumerate(suffix):
        keys[:, (tiles + d) * rows : (tiles + d + 1) * rows] = ref[...]
        key_pos = ((sub_ref[0] + len(suffix) - d) % len(suffix)) * rows + iota((rows, rows), 1)
        allowed = (key_pos >= start) & (key_pos <= pos)
        bias[:, d * rows : (d + 1) * rows] = jnp.where(allowed, 0.0, FLOOR_SCORE)
    cut = tiles * rows
    pair = 2
    mask = jnp.concatenate([bias[...]] * pair, axis=0)

    def score(i):
        query = query_buf[i * pair : (i + 1) * pair].reshape(pair * rows, width)
        return dot(query, keys[:, :cut]), dot(query, keys[:, cut:]) + mask

    def attend(early, late):
        row_top = jnp.maximum(
            jnp.max(early, axis=1, keepdims=True), jnp.max(late, axis=1, keepdims=True)
        )
        early = jnp.exp2((early - row_top) * score_scale)
        late = jnp.exp2((late - row_top) * score_scale)
        denominator = jnp.sum(early, axis=1, keepdims=True) + jnp.sum(late, axis=1, keepdims=True)
        weighted = dot_nt(early.astype(BF16), keys[:lat, :cut]) + dot_nt(
            late.astype(BF16), keys[:lat, cut:]
        )
        return (weighted / denominator).astype(BF16)

    latent_out = []
    copies[0].wait()
    current = score(0)
    for i in range(heads // pair):
        following = score(i + 1) if i + 1 < heads // pair else None
        latent_out.append(attend(*current))
        current = following
    copies[1].wait()
    head_out = jnp.concatenate(
        [
            dot(latent_out[h // pair][h % pair * rows : (h % pair + 1) * rows], wv_ref[h]).astype(BF16)
            for h in range(heads)
        ],
        axis=1,
    )
    copies[2].wait()
    copies[3].wait()
    x = tokens_ref[...].astype(F32) + dot(head_out, wo_ref[...])
    residual_ref[...] = x
    scale = lax.rsqrt(jnp.mean(x * x, axis=-1, keepdims=True) + EPSILON)
    mid = (x * scale * gain_ref[...]).astype(BF16)
    mid_ref[...] = mid
    copies[4].wait()
    out_ref[...] = dot(place_ref[...], mid).astype(BF16)


def place_kernel(place_ref, mid_ref, out_ref):
    out_ref[...] = dot(place_ref[...], mid_ref[...]).astype(BF16)


def expert_kernel(x_ref, g0, u0, d0, g1, u1, d1, out_ref, buf, activated, sems):
    copies = [
        pltpu.make_async_copy(src, buf.at[i], sems.at[i])
        for i, src in enumerate((g0, u0, g1, u1, d0, d1))
    ]
    for copy in copies:
        copy.start()
    step = 256
    blocks = x_ref.shape[0] // step
    for half in range(2):
        copies[2 * half].wait()
        copies[2 * half + 1].wait()

        @pl.loop(0, blocks)
        def _(i):
            at = pl.ds(pl.multiple_of(i * step, step), step)
            gate = dot_nt(x_ref[at], buf[2 * half])
            up = dot_nt(x_ref[at], buf[2 * half + 1])
            activated[half, at] = (gate / (1.0 + jnp.exp(-gate)) * up).astype(BF16)

    copies[4].wait()
    copies[5].wait()

    @pl.loop(0, blocks)
    def _(i):
        at = pl.ds(pl.multiple_of(i * step, step), step)
        total = dot(activated[0, at], buf[4])
        out_ref[at] = (total + dot(activated[1, at], buf[5])).astype(BF16)


def mix_kernel(base_ref, mix_ref, rows_ref, out_ref):
    rows = base_ref.shape[0]
    width = base_ref.shape[1]
    columns = pl.ds(pl.multiple_of(pl.program_id(0) * width, width), width)
    both = dot(mix_ref[...], rows_ref[:, columns])
    out_ref[...] = (base_ref[...] + (both[:rows] + both[rows:])).astype(out_ref.dtype)


def cost(flops, moved):
    return pl.CostEstimate(flops=int(flops), bytes_accessed=int(moved), transcendentals=0)


SMEM = pl.BlockSpec(memory_space=pltpu.SMEM)
VMEM = pl.BlockSpec(memory_space=pltpu.VMEM)
HBM = pl.BlockSpec(memory_space=pltpu.HBM)


def near_core(x):
    return pltpu.with_memory_space_constraint(x, pltpu.VMEM)


def limit(mebibytes):
    return pltpu.CompilerParams(vmem_limit_bytes=mebibytes << 20)


def whole(array):
    return pl.BlockSpec(array.shape, lambda *_: (0,) * array.ndim)


def layer(
    tokens, attn_gain, w_query, w_latent, latent_gain, w_key_up, w_value_up, w_out, moe_gain,
    w_gate, w_up, w_down, expert_ids, gate_weights, lengths, slab_group, owners, prefix_pool,
):
    rows, model = tokens.shape
    head_count, nope, lat = w_key_up.shape
    width = w_latent.shape[1]
    rope = width - lat
    prefix_len = prefix_pool.shape[1]
    hidden = w_down.shape[1]
    top = expert_ids.shape[1]
    req_count = lax.axis_size("req")
    core_count = lax.axis_size("core")
    sub_count = lax.axis_size("ylo") * core_count
    chips = req_count * lax.axis_size("ylo")
    sub = lax.axis_index("ylo") * core_count + lax.axis_index("core")
    place_info = jnp.stack([sub, jnp.int32(prefix_len)]).astype(jnp.int32)

    quarter_len = prefix_len // sub_count
    quarter = lax.dynamic_slice(prefix_pool[0].T, (0, sub * quarter_len), (width, quarter_len))
    lanes = 128
    piece = width * quarter_len // lanes // req_count
    pieces = (
        quarter.reshape(width, quarter_len // lanes, lanes).transpose(1, 0, 2)
        .reshape(req_count, piece, lanes)
    )
    tag_rows = -piece % 8 or 8
    tag = jnp.broadcast_to(slab_group[0].astype(BF16), (req_count, tag_rows, lanes))
    spread = lax.all_to_all(
        jnp.concatenate([pieces, tag], axis=1), "req", split_axis=0, concat_axis=0, tiled=True
    )
    groups = spread[:, piece, 0].astype(jnp.int32)
    slots = jnp.sum(
        jnp.where(
            groups[:, None] == jnp.arange(owners.shape[0], dtype=jnp.int32)[None, :], owners[None, :], 0
        ),
        axis=1,
    )
    picked = jnp.take(spread, slots, axis=0, mode="clip")
    ylo_count = lax.axis_size("ylo")
    doubled = jnp.broadcast_to(picked[:, None], (req_count, ylo_count) + picked.shape[1:])
    near = lax.all_to_all(
        doubled.reshape((chips,) + picked.shape[1:]), CHIP, split_axis=0, concat_axis=0, tiled=True
    )
    near = near[:, :piece].reshape(req_count, ylo_count, piece, lanes).transpose(1, 0, 2, 3)
    near = near.reshape(ylo_count * quarter_len // lanes, width, lanes)
    swap = [(0, 1), (1, 0)]
    far = lax.ppermute(near, "core", swap)

    gate_t = w_gate[0].T
    up_t = w_up[0].T
    down = w_down[0]
    gate_far = lax.ppermute(gate_t, "core", swap)
    up_far = lax.ppermute(up_t, "core", swap)
    down_far = lax.ppermute(down, "core", swap)

    pair = 2
    steps = head_count // pair
    inverse = (10000.0 ** (-np.arange(rope // 2) / (rope // 2))).astype(np.float32)
    inverse = jnp.broadcast_to(jnp.asarray(inverse)[:, None], (rope // 2, rows))
    w_latent_t = w_latent.T
    gain_row = attn_gain[None, :]
    lgain_row = latent_gain[None, :]
    cache_t, normed, angle = pl.pallas_call(
        cache_kernel,
        name="cache",
        in_specs=[SMEM, SMEM] + [VMEM] * 5,
        out_specs=[VMEM, VMEM, VMEM],
        out_shape=[
            pltpu.HBM((width, rows), BF16),
            pltpu.HBM((rows, model), BF16),
            pltpu.HBM((rows, rope), F32),
        ],
        cost_estimate=cost(2 * rows * model * width, 4e6),
    )(lengths, place_info, tokens, gain_row, w_latent_t, lgain_row, inverse)
    query_full = pl.pallas_call(
        query_kernel,
        name="query",
        grid=(steps,),
        in_specs=[
            whole(normed), whole(angle),
            pl.BlockSpec((model, pair * (nope + rope)), lambda i: (0, i)),
            pl.BlockSpec((pair, nope, lat), lambda i: (i, 0, 0)),
        ],
        out_specs=pl.BlockSpec((pair, rows, width), lambda i: (i, 0, 0)),
        out_shape=pltpu.HBM((head_count, rows, width), BF16),
        cost_estimate=cost(2 * rows * model * w_query.shape[1], 9e6),
    )(normed, angle, w_query, w_key_up)

    back = [
        lax.ppermute(cache_t, ("ylo", "core"), [(k, (k + d) % sub_count) for k in range(sub_count)])
        for d in range(1, sub_count)
    ]

    slot_count = 4 * rows * top // 3
    part_slots = slot_count // PARTS
    depth = part_slots // chips
    ids_t = expert_ids.T
    gates_t = gate_weights.T
    placing = pl.pallas_call(
        functools.partial(route_kernel, depth),
        name="route",
        in_specs=[whole(ids_t)],
        out_specs=VMEM,
        out_shape=pltpu.HBM((PARTS, part_slots, rows), BF16),
        cost_estimate=cost(1e9, 2e6),
    )(ids_t)
    mixing = []
    for part in range(PARTS):
        mixing.append(pl.pallas_call(
            functools.partial(gate_kernel, depth, part),
            name="gates",
            in_specs=[whole(ids_t), whole(gates_t), VMEM],
            out_specs=VMEM,
            out_shape=pltpu.HBM((2 * rows, part_slots), BF16),
            cost_estimate=cost(1e9, 2e6),
        )(ids_t, gates_t, placing))

    moe_row = moe_gain[None, :]
    residual, mid, first_out = pl.pallas_call(
        functools.partial(attend_kernel, (nope + rope) ** (-0.5) * math.log2(math.e)),
        name="attend",
        in_specs=[SMEM, SMEM, HBM] + [VMEM] * 7 + [HBM] * 4,
        out_specs=[VMEM, VMEM, VMEM],
        out_shape=[
            pltpu.HBM((rows, model), F32),
            pltpu.HBM((rows, model), BF16),
            pltpu.HBM((part_slots, model), BF16),
        ],
        scratch_shapes=[
            pltpu.VMEM((width, prefix_len + rows * sub_count), BF16),
            pltpu.VMEM((rows, rows * sub_count), F32),
            pltpu.VMEM(query_full.shape, BF16),
            pltpu.VMEM(w_value_up.shape, BF16),
            pltpu.VMEM(w_out.shape, BF16),
            pltpu.VMEM(tokens.shape, BF16),
            pltpu.VMEM((part_slots, rows), BF16),
            pltpu.SemaphoreType.DMA((5,)),
        ],
        compiler_params=limit(54),
        cost_estimate=cost(5e9, 6e6),
    )(
        lengths, place_info, query_full, cache_t, *map(near_core, (*back, near, far)),
        moe_row, w_value_up, w_out, tokens, placing,
    )

    def exchange(x):
        x = x.reshape(chips, depth, model)
        x = lax.all_to_all(x, CHIP, split_axis=0, concat_axis=0, tiled=True)
        return x.reshape(part_slots, model)

    def place(part):
        return pl.pallas_call(
            place_kernel,
            name="place",
            grid=(2,),
            in_specs=[
                pl.BlockSpec((None, part_slots // 2, rows), lambda i: (part, i, 0)), VMEM,
            ],
            out_specs=pl.BlockSpec((part_slots // 2, model), lambda i: (i, 0)),
            out_shape=pltpu.HBM((part_slots, model), BF16),
            cost_estimate=cost(2 * part_slots * rows * model, 3e6),
        )(placing, mid)

    def experts(x):
        return pl.pallas_call(
            expert_kernel,
            name="experts",
            in_specs=[VMEM] + [HBM] * 6,
            out_specs=pl.BlockSpec((part_slots, model), lambda: (0, 0)),
            out_shape=pltpu.HBM((part_slots, model), BF16),
            scratch_shapes=[
                pltpu.VMEM((6, hidden, model), BF16), pltpu.VMEM((2, part_slots, hidden), BF16),
                pltpu.SemaphoreType.DMA((6,)),
            ],
            compiler_params=limit(54),
            cost_estimate=cost(12 * part_slots * model * hidden, 21e6),
        )(near_core(x), gate_t, up_t, down, gate_far, up_far, down_far)

    blocks = 4

    def mix(base, part, x, last):
        shape = (rows, model)
        return pl.pallas_call(
            mix_kernel,
            name="mix",
            grid=(blocks,),
            in_specs=[pl.BlockSpec((rows, model // blocks), lambda i: (0, i)), VMEM, VMEM],
            out_specs=pl.BlockSpec((rows, model // blocks), lambda i: (0, i)),
            out_shape=pltpu.HBM(shape, BF16 if last else F32),
            compiler_params=limit(54),
            cost_estimate=cost(4 * part_slots * rows * model, 3e6),
        )(base, mixing[part], near_core(x))

    outbound = [first_out] + [place(part) for part in range(1, PARTS)]
    arrived = [exchange(x) for x in outbound]
    returned = [exchange(experts(x)) for x in arrived]
    total = residual
    for part in range(PARTS):
        total = mix(total, part, returned[part], part == PARTS - 1)
    return (total, cache_t.T)


def solution(mesh):
    split = Mesh(mesh.devices.reshape(mesh.devices.shape[0], -1, 2), ("req", "ylo", "core"))
    every = ("req", "ylo", "core")
    in_specs = (
        P(every, None), P(), P(), P(), P(), P(), P(), P(), P(),
        P(every, None, None), P(every, None, None), P(every, None, None),
        P(every, None), P(every, None), P("req", None), P("req"), P(), P("req", None, None),
    )
    out_specs = (P(every, None), P(every, None))
    return jax.shard_map(layer, mesh=split, in_specs=in_specs, out_specs=out_specs, check_vma=False)
```

```python
import functools
import math

import jax
import jax.numpy as jnp
import numpy as np
from jax import lax
from jax.experimental import pallas as pl
from jax.experimental.pallas import tpu as pltpu
from jax.sharding import Mesh
from jax.sharding import PartitionSpec as P


EPSILON = 1e-06
FLOOR_SCORE = -1e30
PARTS = 2
CHIP = ("req", "ylo")
BF16 = jnp.bfloat16
F32 = jnp.float32
NT = (((1,), (1,)), ((), ()))


def dot(a, b):
    return jnp.dot(a, b, preferred_element_type=F32)


def dot_nt(a, b):
    return lax.dot_general(a, b, NT, preferred_element_type=F32)


def iota(shape, axis):
    return lax.broadcasted_iota(jnp.int32, shape, axis)


def seg_starts(lengths_ref, pos):
    end_0 = lengths_ref[0, 0]
    end_1 = end_0 + lengths_ref[0, 1]
    return jnp.where(pos >= end_1, end_1, jnp.where(pos >= end_0, end_0, 0))


def spread_matrix(part_slots, experts):
    owner = iota((part_slots, experts), 0) // (part_slots // experts)
    return jnp.where(owner == iota((part_slots, experts), 1), 1.0, 0.0).astype(BF16)


def route_kernel(depth, ids_ref, place_ref):
    top, rows = ids_ref.shape
    parts, part_slots, _ = place_ref.shape
    experts = part_slots // depth
    e_iota = iota((experts, rows), 0)
    named = jnp.zeros((experts, rows), F32)
    for k in range(top):
        named = named + jnp.where(ids_ref[k : k + 1, :] == e_iota, 1.0, 0.0)
    before = jnp.where(iota((rows, rows), 0) < iota((rows, rows), 1), 1.0, 0.0).astype(BF16)
    rank = dot(named.astype(BF16), before)
    order = (named * (rank + 1.0)).astype(BF16)
    order_at = dot(spread_matrix(part_slots, experts), order)
    level = (iota((part_slots, rows), 0) % depth).astype(F32)
    for part in range(parts):
        put = order_at == level + (1.0 + part * depth)
        place_ref[part] = jnp.where(put, 1.0, 0.0).astype(BF16)


def gate_kernel(depth, part, ids_ref, gates_ref, place_ref, mix_ref):
    top, rows = ids_ref.shape
    part_slots = place_ref.shape[1]
    experts = part_slots // depth
    e_iota = iota((experts, rows), 0)
    gate = jnp.zeros((experts, rows), F32)
    for k in range(top):
        gate = gate + jnp.where(ids_ref[k : k + 1, :] == e_iota, gates_ref[k : k + 1, :], 0.0)
    gate_high = gate.astype(BF16)
    gate_low = (gate - gate_high.astype(F32)).astype(BF16)
    spread = spread_matrix(part_slots, experts)
    put = place_ref[part].astype(F32) > 0.5
    mix_ref[:rows] = jnp.where(put, dot(spread, gate_high), 0.0).T.astype(BF16)
    mix_ref[rows:] = jnp.where(put, dot(spread, gate_low), 0.0).T.astype(BF16)


def cache_kernel(
    lengths_ref, sub_ref, tokens_ref, gain_ref, wl_ref, lgain_ref, inverse_ref,
    cache_ref, normed_ref, angle_ref,
):
    rows = tokens_ref.shape[0]
    lat = lgain_ref.shape[1]
    half = (wl_ref.shape[0] - lat) // 2
    x = tokens_ref[...].astype(F32)
    scale = lax.rsqrt(jnp.mean(x * x, axis=-1, keepdims=True) + EPSILON)
    normed = (x * scale * gain_ref[...]).astype(BF16)
    normed_ref[...] = normed
    pos = sub_ref[0] * rows + iota((half, rows), 1)
    offset = sub_ref[1] + pos - seg_starts(lengths_ref, pos)
    angles = offset.astype(F32) * inverse_ref[...]
    cos_part = jnp.cos(angles)
    sin_part = jnp.sin(angles)
    angle_ref[...] = jnp.concatenate([cos_part, sin_part], axis=0).T
    latent = dot_nt(wl_ref[...], normed)
    low = latent[:lat]
    scale = lax.rsqrt(jnp.mean(low * low, axis=0, keepdims=True) + EPSILON)
    gain = jnp.broadcast_to(lgain_ref[...], (rows, lat)).T
    cache_ref[:lat] = (low * scale * gain).astype(BF16)
    first = latent[lat : lat + half]
    second = latent[lat + half :]
    cache_ref[lat : lat + half] = (first * cos_part - second * sin_part).astype(BF16)
    cache_ref[lat + half :] = (second * cos_part + first * sin_part).astype(BF16)


def query_kernel(normed_ref, angle_ref, wq_ref, wk_ref, query_ref):
    heads, nope, lat = wk_ref.shape
    rope = angle_ref.shape[1]
    half = rope // 2
    queries = dot(normed_ref[...], wq_ref[...]).astype(BF16)
    cos_part = angle_ref[:, :half]
    sin_part = angle_ref[:, half:]
    for h in range(heads):
        base = h * (nope + rope)
        query_ref[h, :, :lat] = dot(queries[:, base : base + nope], wk_ref[h]).astype(BF16)
        first = queries[:, base + nope : base + nope + half].astype(F32)
        second = queries[:, base + nope + half : base + nope + rope].astype(F32)
        query_ref[h, :, lat:] = jnp.concatenate(
            [first * cos_part - second * sin_part, second * cos_part + first * sin_part], axis=1
        ).astype(BF16)


PAIR = 2


def late_kernel(
    score_scale, lengths_ref, sub_ref, query_ref, own_ref, back_1_ref, back_2_ref, back_3_ref,
    weighted_ref, stats_ref, keys, bias,
):
    heads, rows, width = query_ref.shape
    lat = weighted_ref.shape[1]
    suffix = (own_ref, back_1_ref, back_2_ref, back_3_ref)
    pos = sub_ref[0] * rows + iota((rows, rows), 0)
    start = seg_starts(lengths_ref, pos)
    for d, ref in enumerate(suffix):
        at = slice(d * rows, (d + 1) * rows)
        keys[:, at] = ref[...]
        key_pos = ((sub_ref[0] + len(suffix) - d) % len(suffix)) * rows + iota((rows, rows), 1)
        allowed = (key_pos >= start) & (key_pos <= pos)
        bias[:, at] = jnp.where(allowed, 0.0, FLOOR_SCORE)
    mask = jnp.concatenate([bias[...]] * PAIR, axis=0)
    count = PAIR * rows
    lane = iota((count, stats_ref.shape[1]), 1)

    def score(i):
        query = query_ref[i * PAIR : (i + 1) * PAIR].reshape(count, width)
        return dot(query, keys[...]) + mask

    current = score(0)
    for i in range(heads // PAIR):
        following = score(i + 1) if i + 1 < heads // PAIR else None
        at = slice(i * count, (i + 1) * count)
        row_top = jnp.max(current, axis=1, keepdims=True)
        weights = jnp.exp2((current - row_top) * score_scale)
        denominator = jnp.sum(weights, axis=1, keepdims=True)
        weighted_ref[at] = dot_nt(weights.astype(BF16), keys[:lat])
        stats_ref[at] = jnp.where(lane == 0, row_top, denominator)
        current = following


def attend_kernel(
    score_scale, query_hbm, late_hbm, stats_hbm, near_ref, far_ref, gain_ref,
    wv_hbm, wo_hbm, tokens_hbm, place_hbm,
    residual_hbm, mid_hbm, out_hbm,
    keys, query_ref, late_ref, stats_ref, wv_ref, wo_ref, tokens_ref, place_ref,
    residual_ref, mid_ref, out_ref, sems,
):
    copies = [
        pltpu.make_async_copy(src, dst, sems.at[i])
        for i, (src, dst) in enumerate((
            (query_hbm, query_ref), (stats_hbm, stats_ref), (late_hbm, late_ref), (wv_hbm, wv_ref),
            (wo_hbm, wo_ref), (tokens_hbm, tokens_ref), (place_hbm.at[0], place_ref),
        ))
    ]
    for copy in copies:
        copy.start()
    rows = tokens_ref.shape[0]
    heads, lat, _ = wv_ref.shape
    width = query_ref.shape[2]
    near_tiles = near_ref.shape[0]
    for i in range(near_tiles):
        keys[:, i * rows : (i + 1) * rows] = near_ref[i]
        keys[:, (near_tiles + i) * rows : (near_tiles + i + 1) * rows] = far_ref[i]
    count = PAIR * rows

    def score(i):
        query = query_ref[i * PAIR : (i + 1) * PAIR].reshape(count, width)
        return dot(query, keys[...])

    def attend(i, early):
        at = slice(i * count, (i + 1) * count)
        late_top = stats_ref[at, 0:1]
        row_top = jnp.maximum(jnp.max(early, axis=1, keepdims=True), late_top)
        early = jnp.exp2((early - row_top) * score_scale)
        share = jnp.exp2((late_top - row_top) * score_scale)
        denominator = jnp.sum(early, axis=1, keepdims=True) + share * stats_ref[at, 1:2]
        weighted = dot_nt(early.astype(BF16), keys[:lat]) + late_ref[at] * share
        return (weighted / denominator).astype(BF16)

    latent_out = []
    copies[0].wait()
    current = score(0)
    copies[1].wait()
    copies[2].wait()
    for i in range(heads // PAIR):
        following = score(i + 1) if i + 1 < heads // PAIR else None
        latent_out.append(attend(i, current))
        current = following
    copies[3].wait()
    head_out = jnp.concatenate(
        [
            dot(latent_out[h // PAIR][h % PAIR * rows : (h % PAIR + 1) * rows], wv_ref[h]).astype(BF16)
            for h in range(heads)
        ],
        axis=1,
    )
    copies[4].wait()
    copies[5].wait()
    x = tokens_ref[...].astype(F32) + dot(head_out, wo_ref[...])
    residual_ref[...] = x
    base = len(copies)
    writes = [pltpu.make_async_copy(residual_ref, residual_hbm, sems.at[base])]
    writes[0].start()
    scale = lax.rsqrt(jnp.mean(x * x, axis=-1, keepdims=True) + EPSILON)
    mid = (x * scale * gain_ref[...]).astype(BF16)
    mid_ref[...] = mid
    writes.append(pltpu.make_async_copy(mid_ref, mid_hbm, sems.at[base + 1]))
    writes[1].start()
    copies[6].wait()
    step = out_ref.shape[0] // 2
    for i in range(2):
        at = slice(i * step, (i + 1) * step)
        out_ref[at] = dot(place_ref[at], mid).astype(BF16)
        writes.append(
            pltpu.make_async_copy(out_ref.at[at], out_hbm.at[at], sems.at[base + 2 + i])
        )
        writes[-1].start()
    for write in writes:
        write.wait()


def place_kernel(place_ref, mid_ref, out_ref):
    out_ref[...] = dot(place_ref[...], mid_ref[...]).astype(BF16)


def expert_kernel(x_ref, g0, u0, d0, g1, u1, d1, out_ref, buf, activated, sems):
    copies = [
        pltpu.make_async_copy(src, buf.at[i], sems.at[i])
        for i, src in enumerate((g0, u0, g1, u1, d0, d1))
    ]
    for copy in copies:
        copy.start()
    step = 256
    blocks = x_ref.shape[0] // step
    for half in range(2):
        copies[2 * half].wait()
        copies[2 * half + 1].wait()

        @pl.loop(0, blocks)
        def _(i):
            at = pl.ds(pl.multiple_of(i * step, step), step)
            gate = dot_nt(x_ref[at], buf[2 * half])
            up = dot_nt(x_ref[at], buf[2 * half + 1])
            activated[half, at] = (gate / (1.0 + jnp.exp(-gate)) * up).astype(BF16)

    copies[4].wait()
    copies[5].wait()

    @pl.loop(0, blocks)
    def _(i):
        at = pl.ds(pl.multiple_of(i * step, step), step)
        total = dot(activated[0, at], buf[4])
        out_ref[at] = (total + dot(activated[1, at], buf[5])).astype(BF16)


def mix_kernel(base_ref, mix_ref, rows_ref, out_ref):
    rows = base_ref.shape[0]
    both = dot(mix_ref[...], rows_ref[...])
    out_ref[...] = (base_ref[...] + (both[:rows] + both[rows:])).astype(out_ref.dtype)


def cost(flops, moved):
    return pl.CostEstimate(flops=int(flops), bytes_accessed=int(moved), transcendentals=0)


SMEM = pl.BlockSpec(memory_space=pltpu.SMEM)
VMEM = pl.BlockSpec(memory_space=pltpu.VMEM)
HBM = pl.BlockSpec(memory_space=pltpu.HBM)


def near_core(x):
    return pltpu.with_memory_space_constraint(x, pltpu.VMEM)


def limit(mebibytes):
    return pltpu.CompilerParams(vmem_limit_bytes=mebibytes << 20)


def whole(array):
    return pl.BlockSpec(array.shape, lambda *_: (0,) * array.ndim)


def layer(
    tokens, attn_gain, w_query, w_latent, latent_gain, w_key_up, w_value_up, w_out, moe_gain,
    w_gate, w_up, w_down, expert_ids, gate_weights, lengths, slab_group, owners, prefix_pool,
):
    rows, model = tokens.shape
    head_count, nope, lat = w_key_up.shape
    width = w_latent.shape[1]
    rope = width - lat
    prefix_len = prefix_pool.shape[1]
    hidden = w_down.shape[1]
    top = expert_ids.shape[1]
    req_count = lax.axis_size("req")
    core_count = lax.axis_size("core")
    sub_count = lax.axis_size("ylo") * core_count
    chips = req_count * lax.axis_size("ylo")
    sub = lax.axis_index("ylo") * core_count + lax.axis_index("core")
    place_info = jnp.stack([sub, jnp.int32(prefix_len)]).astype(jnp.int32)

    quarter_len = prefix_len // sub_count
    quarter = lax.dynamic_slice(prefix_pool[0].T, (0, sub * quarter_len), (width, quarter_len))
    lanes = 128
    piece = width * quarter_len // lanes // req_count
    pieces = (
        quarter.reshape(width, quarter_len // lanes, lanes).transpose(1, 0, 2)
        .reshape(req_count, piece, lanes)
    )
    tag_rows = -piece % 8 or 8
    tag = jnp.broadcast_to(slab_group[0].astype(BF16), (req_count, tag_rows, lanes))
    spread = lax.all_to_all(
        jnp.concatenate([pieces, tag], axis=1), "req", split_axis=0, concat_axis=0, tiled=True
    )
    ylo_count = lax.axis_size("ylo")
    groups = spread[:, piece, 0].astype(jnp.int32)
    slots = jnp.sum(
        jnp.where(
            groups[:, None] == jnp.arange(owners.shape[0], dtype=jnp.int32)[None, :], owners[None, :], 0
        ),
        axis=1,
    )
    picked = jnp.take(spread, jnp.repeat(slots, ylo_count), axis=0, mode="clip")
    near = lax.all_to_all(picked, CHIP, split_axis=0, concat_axis=0, tiled=True)
    near = near[:, :piece].reshape(req_count, ylo_count, piece, lanes).transpose(1, 0, 2, 3)
    near = near.reshape(ylo_count * quarter_len // lanes, width, lanes)
    swap = [(0, 1), (1, 0)]
    far = lax.ppermute(near, "core", swap)

    gate_t = w_gate[0].T
    up_t = w_up[0].T
    down = w_down[0]
    gate_far = lax.ppermute(gate_t, "core", swap)
    up_far = lax.ppermute(up_t, "core", swap)
    down_far = lax.ppermute(down, "core", swap)

    pair = 2
    steps = head_count // pair
    inverse = (10000.0 ** (-np.arange(rope // 2) / (rope // 2))).astype(np.float32)
    inverse = jnp.broadcast_to(jnp.asarray(inverse)[:, None], (rope // 2, rows))
    w_latent_t = w_latent.T
    gain_row = attn_gain[None, :]
    lgain_row = latent_gain[None, :]
    cache_t, normed, angle = pl.pallas_call(
        cache_kernel,
        name="cache",
        in_specs=[SMEM, SMEM] + [VMEM] * 5,
        out_specs=[VMEM, VMEM, VMEM],
        out_shape=[
            pltpu.HBM((width, rows), BF16),
            pltpu.HBM((rows, model), BF16),
            pltpu.HBM((rows, rope), F32),
        ],
        cost_estimate=cost(2 * rows * model * width, 4e6),
    )(lengths, place_info, tokens, gain_row, w_latent_t, lgain_row, inverse)
    query_full = pl.pallas_call(
        query_kernel,
        name="query",
        grid=(steps,),
        in_specs=[
            whole(normed), whole(angle),
            pl.BlockSpec((model, pair * (nope + rope)), lambda i: (0, i)),
            pl.BlockSpec((pair, nope, lat), lambda i: (i, 0, 0)),
        ],
        out_specs=pl.BlockSpec((pair, rows, width), lambda i: (i, 0, 0)),
        out_shape=pltpu.HBM((head_count, rows, width), BF16),
        cost_estimate=cost(2 * rows * model * w_query.shape[1], 9e6),
    )(normed, angle, w_query, w_key_up)

    back = [
        lax.ppermute(cache_t, ("ylo", "core"), [(k, (k + d) % sub_count) for k in range(sub_count)])
        for d in range(1, sub_count)
    ]

    slot_count = 4 * rows * top // 3
    part_slots = slot_count // PARTS
    depth = part_slots // chips
    ids_t = expert_ids.T
    gates_t = gate_weights.T
    placing = pl.pallas_call(
        functools.partial(route_kernel, depth),
        name="route",
        in_specs=[whole(ids_t)],
        out_specs=VMEM,
        out_shape=pltpu.HBM((PARTS, part_slots, rows), BF16),
        cost_estimate=cost(1e9, 2e6),
    )(ids_t)
    mixing = []
    for part in range(PARTS):
        mixing.append(pl.pallas_call(
            functools.partial(gate_kernel, depth, part),
            name="gates",
            in_specs=[whole(ids_t), whole(gates_t), VMEM],
            out_specs=VMEM,
            out_shape=pltpu.HBM((2 * rows, part_slots), BF16),
            cost_estimate=cost(1e9, 2e6),
        )(ids_t, gates_t, placing))

    moe_row = moe_gain[None, :]
    score_scale = (nope + rope) ** (-0.5) * math.log2(math.e)
    lines = head_count * rows
    late, stats = pl.pallas_call(
        functools.partial(late_kernel, score_scale),
        name="late",
        in_specs=[SMEM, SMEM] + [VMEM] * 5,
        out_specs=[VMEM, VMEM],
        out_shape=[pltpu.HBM((lines, lat), F32), pltpu.HBM((lines, 128), F32)],
        scratch_shapes=[
            pltpu.VMEM((width, rows * sub_count), BF16), pltpu.VMEM((rows, rows * sub_count), F32),
        ],
        compiler_params=limit(54),
        cost_estimate=cost(1e9, 6e6),
    )(lengths, place_info, query_full, cache_t, *map(near_core, back))
    residual, mid, first_out = pl.pallas_call(
        functools.partial(attend_kernel, score_scale),
        name="attend",
        in_specs=[HBM] * 3 + [VMEM] * 3 + [HBM] * 4,
        out_specs=[HBM, HBM, HBM],
        out_shape=[
            pltpu.HBM((rows, model), F32),
            pltpu.HBM((rows, model), BF16),
            pltpu.HBM((part_slots, model), BF16),
        ],
        scratch_shapes=[
            pltpu.VMEM((width, prefix_len), BF16),
            pltpu.VMEM(query_full.shape, BF16),
            pltpu.VMEM((lines, lat), F32),
            pltpu.VMEM((lines, 128), F32),
            pltpu.VMEM(w_value_up.shape, BF16),
            pltpu.VMEM(w_out.shape, BF16),
            pltpu.VMEM(tokens.shape, BF16),
            pltpu.VMEM((part_slots, rows), BF16),
            pltpu.VMEM((rows, model), F32),
            pltpu.VMEM((rows, model), BF16),
            pltpu.VMEM((part_slots, model), BF16),
            pltpu.SemaphoreType.DMA((11,)),
        ],
        compiler_params=limit(54),
        cost_estimate=cost(5e9, 6e6),
    )(
        query_full, late, stats, near_core(near), near_core(far),
        moe_row, w_value_up, w_out, tokens, placing,
    )

    def exchange(x):
        x = x.reshape(chips, depth, model)
        x = lax.all_to_all(x, CHIP, split_axis=0, concat_axis=0, tiled=True)
        return x.reshape(part_slots, model)

    def place(part):
        return pl.pallas_call(
            place_kernel,
            name="place",
            grid=(2,),
            in_specs=[
                pl.BlockSpec((None, part_slots // 2, rows), lambda i: (part, i, 0)), VMEM,
            ],
            out_specs=pl.BlockSpec((part_slots // 2, model), lambda i: (i, 0)),
            out_shape=pltpu.HBM((part_slots, model), BF16),
            cost_estimate=cost(2 * part_slots * rows * model, 3e6),
        )(placing, mid)

    def experts(x):
        return pl.pallas_call(
            expert_kernel,
            name="experts",
            in_specs=[VMEM] + [HBM] * 6,
            out_specs=pl.BlockSpec((part_slots, model), lambda: (0, 0)),
            out_shape=pltpu.HBM((part_slots, model), BF16),
            scratch_shapes=[
                pltpu.VMEM((6, hidden, model), BF16), pltpu.VMEM((2, part_slots, hidden), BF16),
                pltpu.SemaphoreType.DMA((6,)),
            ],
            compiler_params=limit(54),
            cost_estimate=cost(12 * part_slots * model * hidden, 21e6),
        )(near_core(x), gate_t, up_t, down, gate_far, up_far, down_far)

    def mix(base, part, x, last):
        shape = (rows, model)
        return pl.pallas_call(
            mix_kernel,
            name="mix",
            in_specs=[VMEM] * 3,
            out_specs=VMEM,
            out_shape=pltpu.HBM(shape, BF16 if last else F32),
            compiler_params=limit(54),
            cost_estimate=cost(4 * part_slots * rows * model, 3e6),
        )(base, mixing[part], near_core(x))

    outbound = [first_out] + [place(part) for part in range(1, PARTS)]
    arrived = [exchange(x) for x in outbound]
    returned = [exchange(experts(x)) for x in arrived]
    total = residual
    for part in range(PARTS):
        total = mix(total, part, returned[part], part == PARTS - 1)
    return (total, cache_t.T)


def solution(mesh):
    split = Mesh(mesh.devices.reshape(mesh.devices.shape[0], -1, 2), ("req", "ylo", "core"))
    every = ("req", "ylo", "core")
    in_specs = (
        P(every, None), P(), P(), P(), P(), P(), P(), P(), P(),
        P(every, None, None), P(every, None, None), P(every, None, None),
        P(every, None), P(every, None), P("req", None), P("req"), P(), P("req", None, None),
    )
    out_specs = (P(every, None), P(every, None))
    return jax.shard_map(layer, mesh=split, in_specs=in_specs, out_specs=out_specs, check_vma=False)
```

```python
import functools
import math

import jax
import jax.numpy as jnp
import numpy as np
from jax import lax
from jax.experimental import pallas as pl
from jax.experimental.pallas import tpu as pltpu
from jax.sharding import Mesh
from jax.sharding import PartitionSpec as P


EPSILON = 1e-06
FLOOR_SCORE = -1e30
PARTS = 2
CHIP = ("req", "ylo")
BF16 = jnp.bfloat16
F32 = jnp.float32
NT = (((1,), (1,)), ((), ()))


def dot(a, b):
    return jnp.dot(a, b, preferred_element_type=F32)


def dot_nt(a, b):
    return lax.dot_general(a, b, NT, preferred_element_type=F32)


def iota(shape, axis):
    return lax.broadcasted_iota(jnp.int32, shape, axis)


def seg_starts(lengths_ref, pos):
    end_0 = lengths_ref[0, 0]
    end_1 = end_0 + lengths_ref[0, 1]
    return jnp.where(pos >= end_1, end_1, jnp.where(pos >= end_0, end_0, 0))


def pack_kernel(sub_ref, tag_ref, pool_hbm, out_ref, quarter, sem):
    width, quarter_len = quarter.shape
    count, held, lanes = out_ref.shape
    start = pl.multiple_of(sub_ref[0] * quarter_len, quarter_len)
    copy = pltpu.make_async_copy(pool_hbm.at[:, pl.ds(start, quarter_len)], quarter, sem)
    copy.start()
    piece = width * quarter_len // lanes // count
    tag = jnp.full((held - piece, lanes), tag_ref[0].astype(F32), F32)
    copy.wait()
    rows = jnp.concatenate(
        [quarter[:, i * lanes : (i + 1) * lanes] for i in range(quarter_len // lanes)], axis=0
    ).astype(F32)
    for j in range(count):
        out_ref[j] = jnp.concatenate([rows[j * piece : (j + 1) * piece], tag], axis=0).astype(BF16)


def spread_matrix(part_slots, experts):
    owner = iota((part_slots, experts), 0) // (part_slots // experts)
    return jnp.where(owner == iota((part_slots, experts), 1), 1.0, 0.0).astype(BF16)


def route_kernel(depth, ids_ref, place_ref):
    top, rows = ids_ref.shape
    parts, part_slots, _ = place_ref.shape
    experts = part_slots // depth
    e_iota = iota((experts, rows), 0)
    named = jnp.zeros((experts, rows), F32)
    for k in range(top):
        named = named + jnp.where(ids_ref[k : k + 1, :] == e_iota, 1.0, 0.0)
    before = jnp.where(iota((rows, rows), 0) < iota((rows, rows), 1), 1.0, 0.0).astype(BF16)
    rank = dot(named.astype(BF16), before)
    order = (named * (rank + 1.0)).astype(BF16)
    order_at = dot(spread_matrix(part_slots, experts), order)
    level = (iota((part_slots, rows), 0) % depth).astype(F32)
    for part in range(parts):
        put = order_at == level + (1.0 + part * depth)
        place_ref[part] = jnp.where(put, 1.0, 0.0).astype(BF16)


def gate_kernel(depth, part, ids_ref, gates_ref, place_ref, mix_ref):
    top, rows = ids_ref.shape
    part_slots = place_ref.shape[1]
    experts = part_slots // depth
    e_iota = iota((experts, rows), 0)
    gate = jnp.zeros((experts, rows), F32)
    for k in range(top):
        gate = gate + jnp.where(ids_ref[k : k + 1, :] == e_iota, gates_ref[k : k + 1, :], 0.0)
    gate_high = gate.astype(BF16)
    gate_low = (gate - gate_high.astype(F32)).astype(BF16)
    spread = spread_matrix(part_slots, experts)
    put = place_ref[part].astype(F32) > 0.5
    mix_ref[:rows] = jnp.where(put, dot(spread, gate_high), 0.0).T.astype(BF16)
    mix_ref[rows:] = jnp.where(put, dot(spread, gate_low), 0.0).T.astype(BF16)


def cache_kernel(
    prefix_len, lengths_ref, sub_ref, tokens_ref, gain_ref, wl_ref, lgain_ref, inverse_ref,
    cache_ref, normed_ref, angle_ref,
):
    rows = tokens_ref.shape[0]
    lat = lgain_ref.shape[1]
    half = (wl_ref.shape[0] - lat) // 2
    x = tokens_ref[...].astype(F32)
    scale = lax.rsqrt(jnp.mean(x * x, axis=-1, keepdims=True) + EPSILON)
    normed = (x * scale * gain_ref[...]).astype(BF16)
    normed_ref[...] = normed
    pos = sub_ref[0] * rows + iota((half, rows), 1)
    offset = prefix_len + pos - seg_starts(lengths_ref, pos)
    angles = offset.astype(F32) * inverse_ref[...]
    cos_part = jnp.cos(angles)
    sin_part = jnp.sin(angles)
    angle_ref[...] = jnp.concatenate([cos_part, sin_part], axis=0).T
    latent = dot_nt(wl_ref[...], normed)
    low = latent[:lat]
    scale = lax.rsqrt(jnp.mean(low * low, axis=0, keepdims=True) + EPSILON)
    gain = jnp.broadcast_to(lgain_ref[...], (rows, lat)).T
    cache_ref[:lat] = (low * scale * gain).astype(BF16)
    first = latent[lat : lat + half]
    second = latent[lat + half :]
    cache_ref[lat : lat + half] = (first * cos_part - second * sin_part).astype(BF16)
    cache_ref[lat + half :] = (second * cos_part + first * sin_part).astype(BF16)


def query_kernel(
    score_scale, lengths_ref, sub_ref, normed_ref, angle_ref, wq_ref, wk_ref,
    own_ref, back_1_ref, back_2_ref, back_3_ref,
    query_ref, weighted_ref, stats_ref, keys, mask,
):
    heads, nope, lat = wk_ref.shape
    rows, rope = angle_ref.shape
    half = rope // 2
    count = heads * rows

    @pl.when(pl.program_id(0) == 0)
    def _():
        suffix = (own_ref, back_1_ref, back_2_ref, back_3_ref)
        pos = sub_ref[0] * rows + iota((rows, rows), 0)
        start = seg_starts(lengths_ref, pos)
        for d, ref in enumerate(suffix):
            at = slice(d * rows, (d + 1) * rows)
            keys[:, at] = ref[...]
            key_pos = ((sub_ref[0] + len(suffix) - d) % len(suffix)) * rows + iota((rows, rows), 1)
            allowed = (key_pos >= start) & (key_pos <= pos)
            floor = jnp.where(allowed, 0.0, FLOOR_SCORE)
            for h in range(heads):
                mask[h * rows : (h + 1) * rows, at] = floor

    queries = dot(normed_ref[...], wq_ref[...]).astype(BF16)
    cos_part = angle_ref[:, :half]
    sin_part = angle_ref[:, half:]
    for h in range(heads):
        base = h * (nope + rope)
        query_ref[h, :, :lat] = dot(queries[:, base : base + nope], wk_ref[h]).astype(BF16)
        first = queries[:, base + nope : base + nope + half].astype(F32)
        second = queries[:, base + nope + half : base + nope + rope].astype(F32)
        query_ref[h, :, lat:] = jnp.concatenate(
            [first * cos_part - second * sin_part, second * cos_part + first * sin_part], axis=1
        ).astype(BF16)
    scores = dot(query_ref[...].reshape(count, lat + rope), keys[...]) + mask[...]
    row_top = jnp.max(scores, axis=1, keepdims=True)
    weights = jnp.exp2((scores - row_top) * score_scale)
    denominator = jnp.sum(weights, axis=1, keepdims=True)
    weighted_ref[...] = dot_nt(weights.astype(BF16), keys[:lat])
    stats_ref[...] = jnp.where(iota(stats_ref.shape, 1) == 0, row_top, denominator)


PAIR = 2


def attend_kernel(
    score_scale, query_hbm, late_hbm, stats_hbm, near_ref, far_ref, gain_ref,
    wv_hbm, wo_hbm, tokens_hbm, place_hbm,
    residual_hbm, mid_hbm, out_hbm,
    keys, query_ref, late_ref, stats_ref, wv_ref, wo_ref, tokens_ref, place_ref,
    residual_ref, mid_ref, out_ref, sems,
):
    copies = [
        pltpu.make_async_copy(src, dst, sems.at[i])
        for i, (src, dst) in enumerate((
            (query_hbm, query_ref), (stats_hbm, stats_ref), (late_hbm, late_ref), (wv_hbm, wv_ref),
            (wo_hbm, wo_ref), (tokens_hbm, tokens_ref), (place_hbm.at[0], place_ref),
        ))
    ]
    for copy in copies:
        copy.start()
    rows = tokens_ref.shape[0]
    heads, lat, _ = wv_ref.shape
    width = query_ref.shape[2]
    near_tiles = near_ref.shape[0]
    for i in range(near_tiles):
        keys[:, i * rows : (i + 1) * rows] = near_ref[i]
        keys[:, (near_tiles + i) * rows : (near_tiles + i + 1) * rows] = far_ref[i]
    count = PAIR * rows

    def score(i):
        query = query_ref[i * PAIR : (i + 1) * PAIR].reshape(count, width)
        return dot(query, keys[...])

    def attend(i, early):
        at = slice(i * count, (i + 1) * count)
        late_top = stats_ref[at, 0:1]
        row_top = jnp.maximum(jnp.max(early, axis=1, keepdims=True), late_top)
        early = jnp.exp2((early - row_top) * score_scale)
        share = jnp.exp2((late_top - row_top) * score_scale)
        denominator = jnp.sum(early, axis=1, keepdims=True) + share * stats_ref[at, 1:2]
        weighted = dot_nt(early.astype(BF16), keys[:lat]) + late_ref[at] * share
        return (weighted / denominator).astype(BF16)

    latent_out = []
    copies[0].wait()
    current = score(0)
    copies[1].wait()
    copies[2].wait()
    for i in range(heads // PAIR):
        following = score(i + 1) if i + 1 < heads // PAIR else None
        latent_out.append(attend(i, current))
        current = following
    copies[3].wait()
    head_out = jnp.concatenate(
        [
            dot(latent_out[h // PAIR][h % PAIR * rows : (h % PAIR + 1) * rows], wv_ref[h]).astype(BF16)
            for h in range(heads)
        ],
        axis=1,
    )
    copies[4].wait()
    copies[5].wait()
    x = tokens_ref[...].astype(F32) + dot(head_out, wo_ref[...])
    residual_ref[...] = x
    base = len(copies)
    writes = [pltpu.make_async_copy(residual_ref, residual_hbm, sems.at[base])]
    writes[0].start()
    scale = lax.rsqrt(jnp.mean(x * x, axis=-1, keepdims=True) + EPSILON)
    mid = (x * scale * gain_ref[...]).astype(BF16)
    mid_ref[...] = mid
    writes.append(pltpu.make_async_copy(mid_ref, mid_hbm, sems.at[base + 1]))
    writes[1].start()
    copies[6].wait()
    step = out_ref.shape[0] // 2
    for i in range(2):
        at = slice(i * step, (i + 1) * step)
        out_ref[at] = dot(place_ref[at], mid).astype(BF16)
        writes.append(
            pltpu.make_async_copy(out_ref.at[at], out_hbm.at[at], sems.at[base + 2 + i])
        )
        writes[-1].start()
    for write in writes:
        write.wait()


def place_kernel(place_ref, mid_ref, out_ref):
    out_ref[...] = dot(place_ref[...], mid_ref[...]).astype(BF16)


def expert_kernel(x_ref, g0, u0, d0, g1, u1, d1, out_ref, buf, activated, sems):
    copies = [
        pltpu.make_async_copy(src, buf.at[i], sems.at[i])
        for i, src in enumerate((g0, u0, g1, u1, d0, d1))
    ]
    for copy in copies:
        copy.start()
    step = 256
    blocks = x_ref.shape[0] // step
    for half in range(2):
        copies[2 * half].wait()
        copies[2 * half + 1].wait()

        @pl.loop(0, blocks)
        def _(i):
            at = pl.ds(pl.multiple_of(i * step, step), step)
            gate = dot_nt(x_ref[at], buf[2 * half])
            up = dot_nt(x_ref[at], buf[2 * half + 1])
            activated[half, at] = (gate / (1.0 + jnp.exp(-gate)) * up).astype(BF16)

    copies[4].wait()
    copies[5].wait()

    @pl.loop(0, blocks)
    def _(i):
        at = pl.ds(pl.multiple_of(i * step, step), step)
        total = dot(activated[0, at], buf[4])
        out_ref[at] = (total + dot(activated[1, at], buf[5])).astype(BF16)


def mix_kernel(base_ref, mix_ref, rows_ref, out_ref):
    rows = base_ref.shape[0]
    both = dot(mix_ref[...], rows_ref[...])
    out_ref[...] = (base_ref[...] + (both[:rows] + both[rows:])).astype(out_ref.dtype)


def cost(flops, moved):
    return pl.CostEstimate(flops=int(flops), bytes_accessed=int(moved), transcendentals=0)


SMEM = pl.BlockSpec(memory_space=pltpu.SMEM)
VMEM = pl.BlockSpec(memory_space=pltpu.VMEM)
HBM = pl.BlockSpec(memory_space=pltpu.HBM)


def near_core(x):
    return pltpu.with_memory_space_constraint(x, pltpu.VMEM)


def limit(mebibytes):
    return pltpu.CompilerParams(vmem_limit_bytes=mebibytes << 20)


def whole(array):
    return pl.BlockSpec(array.shape, lambda *_: (0,) * array.ndim)


def layer(
    tokens, attn_gain, w_query, w_latent, latent_gain, w_key_up, w_value_up, w_out, moe_gain,
    w_gate, w_up, w_down, expert_ids, gate_weights, lengths, slab_group, owners, prefix_pool,
):
    rows, model = tokens.shape
    head_count, nope, lat = w_key_up.shape
    width = w_latent.shape[1]
    rope = width - lat
    prefix_len = prefix_pool.shape[1]
    hidden = w_down.shape[1]
    top = expert_ids.shape[1]
    req_count = lax.axis_size("req")
    core_count = lax.axis_size("core")
    sub_count = lax.axis_size("ylo") * core_count
    chips = req_count * lax.axis_size("ylo")
    sub = lax.axis_index("ylo") * core_count + lax.axis_index("core")
    place_info = jnp.reshape(sub, (1,)).astype(jnp.int32)

    quarter_len = prefix_len // sub_count
    lanes = 128
    piece = width * quarter_len // lanes // req_count
    packed = pl.pallas_call(
        pack_kernel,
        name="pack",
        in_specs=[SMEM, SMEM, HBM],
        out_specs=VMEM,
        out_shape=pltpu.HBM((req_count, piece + (-piece % 8 or 8), lanes), BF16),
        scratch_shapes=[pltpu.VMEM((width, quarter_len), BF16), pltpu.SemaphoreType.DMA],
    )(place_info, slab_group, prefix_pool[0].T)
    spread = lax.all_to_all(
        packed, "req", split_axis=0, concat_axis=0, tiled=True
    )
    ylo_count = lax.axis_size("ylo")
    groups = spread[:, piece, 0].astype(jnp.int32)
    slots = jnp.sum(
        jnp.where(
            groups[:, None] == jnp.arange(owners.shape[0], dtype=jnp.int32)[None, :], owners[None, :], 0
        ),
        axis=1,
    )
    picked = jnp.take(spread, jnp.repeat(slots, ylo_count), axis=0, mode="clip")
    near = lax.all_to_all(picked, CHIP, split_axis=0, concat_axis=0, tiled=True)
    near = near[:, :piece].reshape(req_count, ylo_count, piece, lanes).transpose(1, 0, 2, 3)
    near = near.reshape(ylo_count * quarter_len // lanes, width, lanes)
    swap = [(0, 1), (1, 0)]
    far = lax.ppermute(near, "core", swap)

    gate_t = w_gate[0].T
    up_t = w_up[0].T
    down = w_down[0]
    gate_far = lax.ppermute(gate_t, "core", swap)
    up_far = lax.ppermute(up_t, "core", swap)
    down_far = lax.ppermute(down, "core", swap)

    pair = 2
    steps = head_count // pair
    inverse = (10000.0 ** (-np.arange(rope // 2) / (rope // 2))).astype(np.float32)
    inverse = jnp.asarray(np.ascontiguousarray(np.broadcast_to(inverse[:, None], (rope // 2, rows))))
    w_latent_t = w_latent.T
    gain_row = attn_gain[None, :]
    lgain_row = latent_gain[None, :]
    cache_t, normed, angle = pl.pallas_call(
        functools.partial(cache_kernel, prefix_len),
        name="cache",
        in_specs=[SMEM, SMEM] + [VMEM] * 5,
        out_specs=[VMEM, VMEM, VMEM],
        out_shape=[
            pltpu.HBM((width, rows), BF16),
            pltpu.HBM((rows, model), BF16),
            pltpu.HBM((rows, rope), F32),
        ],
        cost_estimate=cost(2 * rows * model * width, 4e6),
    )(lengths, place_info, tokens, gain_row, w_latent_t, lgain_row, inverse)
    back = [
        lax.ppermute(cache_t, ("ylo", "core"), [(k, (k + d) % sub_count) for k in range(sub_count)])
        for d in range(1, sub_count)
    ]

    score_scale = (nope + rope) ** (-0.5) * math.log2(math.e)
    lines = head_count * rows
    query_full, late, stats = pl.pallas_call(
        functools.partial(query_kernel, score_scale),
        name="query",
        grid=(steps,),
        in_specs=[
            SMEM, SMEM, whole(normed), whole(angle),
            pl.BlockSpec((model, pair * (nope + rope)), lambda i: (0, i)),
            pl.BlockSpec((pair, nope, lat), lambda i: (i, 0, 0)),
            VMEM, VMEM, VMEM, VMEM,
        ],
        out_specs=[
            pl.BlockSpec((pair, rows, width), lambda i: (i, 0, 0)),
            pl.BlockSpec((pair * rows, lat), lambda i: (i, 0)),
            pl.BlockSpec((pair * rows, 128), lambda i: (i, 0)),
        ],
        out_shape=[
            pltpu.HBM((head_count, rows, width), BF16),
            pltpu.HBM((lines, lat), F32),
            pltpu.HBM((lines, 128), F32),
        ],
        scratch_shapes=[
            pltpu.VMEM((width, rows * sub_count), BF16),
            pltpu.VMEM((pair * rows, rows * sub_count), F32),
        ],
        compiler_params=limit(54),
        cost_estimate=cost(3e9, 12e6),
    )(
        lengths, place_info, normed, angle, w_query, w_key_up, cache_t, *map(near_core, back),
    )

    slot_count = 4 * rows * top // 3
    part_slots = slot_count // PARTS
    depth = part_slots // chips
    ids_t = expert_ids.T
    gates_t = gate_weights.T
    placing = pl.pallas_call(
        functools.partial(route_kernel, depth),
        name="route",
        in_specs=[whole(ids_t)],
        out_specs=VMEM,
        out_shape=pltpu.HBM((PARTS, part_slots, rows), BF16),
        cost_estimate=cost(1e9, 2e6),
    )(ids_t)
    mixing = []
    for part in range(PARTS):
        mixing.append(pl.pallas_call(
            functools.partial(gate_kernel, depth, part),
            name="gates",
            in_specs=[whole(ids_t), whole(gates_t), VMEM],
            out_specs=VMEM,
            out_shape=pltpu.HBM((2 * rows, part_slots), BF16),
            cost_estimate=cost(1e9, 2e6),
        )(ids_t, gates_t, placing))

    moe_row = moe_gain[None, :]
    residual, mid, first_out = pl.pallas_call(
        functools.partial(attend_kernel, score_scale),
        name="attend",
        in_specs=[HBM] * 3 + [VMEM] * 3 + [HBM] * 4,
        out_specs=[HBM, HBM, HBM],
        out_shape=[
            pltpu.HBM((rows, model), F32),
            pltpu.HBM((rows, model), BF16),
            pltpu.HBM((part_slots, model), BF16),
        ],
        scratch_shapes=[
            pltpu.VMEM((width, prefix_len), BF16),
            pltpu.VMEM(query_full.shape, BF16),
            pltpu.VMEM((lines, lat), F32),
            pltpu.VMEM((lines, 128), F32),
            pltpu.VMEM(w_value_up.shape, BF16),
            pltpu.VMEM(w_out.shape, BF16),
            pltpu.VMEM(tokens.shape, BF16),
            pltpu.VMEM((part_slots, rows), BF16),
            pltpu.VMEM((rows, model), F32),
            pltpu.VMEM((rows, model), BF16),
            pltpu.VMEM((part_slots, model), BF16),
            pltpu.SemaphoreType.DMA((11,)),
        ],
        compiler_params=limit(54),
        cost_estimate=cost(5e9, 6e6),
    )(
        query_full, late, stats, near_core(near), near_core(far),
        moe_row, w_value_up, w_out, tokens, placing,
    )

    def exchange(x):
        x = x.reshape(chips, depth, model)
        x = lax.all_to_all(x, CHIP, split_axis=0, concat_axis=0, tiled=True)
        return x.reshape(part_slots, model)

    def place(part):
        return pl.pallas_call(
            place_kernel,
            name="place",
            grid=(2,),
            in_specs=[
                pl.BlockSpec((None, part_slots // 2, rows), lambda i: (part, i, 0)), VMEM,
            ],
            out_specs=pl.BlockSpec((part_slots // 2, model), lambda i: (i, 0)),
            out_shape=pltpu.HBM((part_slots, model), BF16),
            cost_estimate=cost(2 * part_slots * rows * model, 3e6),
        )(placing, mid)

    def experts(x):
        return pl.pallas_call(
            expert_kernel,
            name="experts",
            in_specs=[VMEM] + [HBM] * 6,
            out_specs=pl.BlockSpec((part_slots, model), lambda: (0, 0)),
            out_shape=pltpu.HBM((part_slots, model), BF16),
            scratch_shapes=[
                pltpu.VMEM((6, hidden, model), BF16), pltpu.VMEM((2, part_slots, hidden), BF16),
                pltpu.SemaphoreType.DMA((6,)),
            ],
            compiler_params=limit(54),
            cost_estimate=cost(12 * part_slots * model * hidden, 21e6),
        )(near_core(x), gate_t, up_t, down, gate_far, up_far, down_far)

    def mix(base, part, x, last):
        shape = (rows, model)
        return pl.pallas_call(
            mix_kernel,
            name="mix",
            in_specs=[VMEM] * 3,
            out_specs=VMEM,
            out_shape=pltpu.HBM(shape, BF16 if last else F32),
            compiler_params=limit(54),
            cost_estimate=cost(4 * part_slots * rows * model, 3e6),
        )(base, mixing[part], near_core(x))

    outbound = [first_out] + [place(part) for part in range(1, PARTS)]
    arrived = [exchange(x) for x in outbound]
    returned = [exchange(experts(x)) for x in arrived]
    total = residual
    for part in range(PARTS):
        total = mix(total, part, returned[part], part == PARTS - 1)
    return (total, cache_t.T)


def solution(mesh):
    split = Mesh(mesh.devices.reshape(mesh.devices.shape[0], -1, 2), ("req", "ylo", "core"))
    every = ("req", "ylo", "core")
    in_specs = (
        P(every, None), P(), P(), P(), P(), P(), P(), P(), P(),
        P(every, None, None), P(every, None, None), P(every, None, None),
        P(every, None), P(every, None), P("req", None), P("req"), P(), P("req", None, None),
    )
    out_specs = (P(every, None), P(every, None))
    return jax.shard_map(layer, mesh=split, in_specs=in_specs, out_specs=out_specs, check_vma=False)
```

```python
import functools
import math

import jax
import jax.numpy as jnp
import numpy as np
from jax import lax
from jax.experimental import pallas as pl
from jax.experimental.pallas import tpu as pltpu
from jax.sharding import Mesh
from jax.sharding import PartitionSpec as P


EPSILON = 1e-06
FLOOR_SCORE = -1e30
PARTS = 2
CHIP = ("req", "ylo")
BF16 = jnp.bfloat16
F32 = jnp.float32
NT = (((1,), (1,)), ((), ()))


def dot(a, b):
    return jnp.dot(a, b, preferred_element_type=F32)


def dot_nt(a, b):
    return lax.dot_general(a, b, NT, preferred_element_type=F32)


def iota(shape, axis):
    return lax.broadcasted_iota(jnp.int32, shape, axis)


def seg_starts(lengths_ref, pos):
    end_0 = lengths_ref[0, 0]
    end_1 = end_0 + lengths_ref[0, 1]
    return jnp.where(pos >= end_1, end_1, jnp.where(pos >= end_0, end_0, 0))


def pack_kernel(sub_ref, tag_ref, pool_hbm, out_ref, quarter, sem):
    width, quarter_len = quarter.shape
    count, held, lanes = out_ref.shape
    start = pl.multiple_of(sub_ref[0] * quarter_len, quarter_len)
    copy = pltpu.make_async_copy(pool_hbm.at[:, pl.ds(start, quarter_len)], quarter, sem)
    copy.start()
    piece = width * quarter_len // lanes // count
    tag = jnp.full((held - piece, lanes), tag_ref[0].astype(F32), F32)
    copy.wait()
    rows = jnp.concatenate(
        [quarter[:, i * lanes : (i + 1) * lanes] for i in range(quarter_len // lanes)], axis=0
    ).astype(F32)
    for j in range(count):
        out_ref[j] = jnp.concatenate([rows[j * piece : (j + 1) * piece], tag], axis=0).astype(BF16)


def spread_matrix(part_slots, experts):
    owner = iota((part_slots, experts), 0) // (part_slots // experts)
    return jnp.where(owner == iota((part_slots, experts), 1), 1.0, 0.0).astype(BF16)


def route_kernel(depth, ids_ref, place_ref):
    top, rows = ids_ref.shape
    parts, part_slots, _ = place_ref.shape
    experts = part_slots // depth
    e_iota = iota((experts, rows), 0)
    named = jnp.zeros((experts, rows), F32)
    for k in range(top):
        named = named + jnp.where(ids_ref[k : k + 1, :] == e_iota, 1.0, 0.0)
    before = jnp.where(iota((rows, rows), 0) < iota((rows, rows), 1), 1.0, 0.0).astype(BF16)
    rank = dot(named.astype(BF16), before)
    order = (named * (rank + 1.0)).astype(BF16)
    order_at = dot(spread_matrix(part_slots, experts), order)
    level = (iota((part_slots, rows), 0) % depth).astype(F32)
    for part in range(parts):
        put = order_at == level + (1.0 + part * depth)
        place_ref[part] = jnp.where(put, 1.0, 0.0).astype(BF16)


def gate_kernel(depth, part, ids_ref, gates_ref, place_ref, mix_ref):
    top, rows = ids_ref.shape
    part_slots = place_ref.shape[1]
    experts = part_slots // depth
    e_iota = iota((experts, rows), 0)
    gate = jnp.zeros((experts, rows), F32)
    for k in range(top):
        gate = gate + jnp.where(ids_ref[k : k + 1, :] == e_iota, gates_ref[k : k + 1, :], 0.0)
    gate_high = gate.astype(BF16)
    gate_low = (gate - gate_high.astype(F32)).astype(BF16)
    spread = spread_matrix(part_slots, experts)
    put = place_ref[part].astype(F32) > 0.5
    mix_ref[:rows] = jnp.where(put, dot(spread, gate_high), 0.0).T.astype(BF16)
    mix_ref[rows:] = jnp.where(put, dot(spread, gate_low), 0.0).T.astype(BF16)


def cache_kernel(
    prefix_len, lengths_ref, sub_ref, tokens_ref, gain_ref, wl_hbm, lgain_ref, inverse_ref,
    cache_ref, normed_ref, angle_ref, wl_ref, sem,
):
    copy = pltpu.make_async_copy(wl_hbm, wl_ref, sem)
    copy.start()
    rows = tokens_ref.shape[0]
    lat = lgain_ref.shape[1]
    half = (wl_ref.shape[0] - lat) // 2
    x = tokens_ref[...].astype(F32)
    scale = lax.rsqrt(jnp.mean(x * x, axis=-1, keepdims=True) + EPSILON)
    normed = (x * scale * gain_ref[...]).astype(BF16)
    normed_ref[...] = normed
    pos = sub_ref[0] * rows + iota((half, rows), 1)
    offset = prefix_len + pos - seg_starts(lengths_ref, pos)
    angles = offset.astype(F32) * inverse_ref[...]
    cos_part = jnp.cos(angles)
    sin_part = jnp.sin(angles)
    angle_ref[...] = jnp.concatenate([cos_part, sin_part], axis=0).T
    copy.wait()
    latent = dot_nt(wl_ref[...], normed)
    low = latent[:lat]
    scale = lax.rsqrt(jnp.mean(low * low, axis=0, keepdims=True) + EPSILON)
    gain = jnp.broadcast_to(lgain_ref[...], (rows, lat)).T
    cache_ref[:lat] = (low * scale * gain).astype(BF16)
    first = latent[lat : lat + half]
    second = latent[lat + half :]
    cache_ref[lat : lat + half] = (first * cos_part - second * sin_part).astype(BF16)
    cache_ref[lat + half :] = (second * cos_part + first * sin_part).astype(BF16)


def query_kernel(
    score_scale, lengths_ref, sub_ref, normed_ref, angle_ref, wq_ref, wk_ref,
    own_ref, back_1_ref, back_2_ref, back_3_ref,
    query_ref, weighted_ref, stats_ref, keys, mask,
):
    heads, nope, lat = wk_ref.shape
    rows, rope = angle_ref.shape
    half = rope // 2
    count = heads * rows

    @pl.when(pl.program_id(0) == 0)
    def _():
        suffix = (own_ref, back_1_ref, back_2_ref, back_3_ref)
        pos = sub_ref[0] * rows + iota((rows, rows), 0)
        start = seg_starts(lengths_ref, pos)
        for d, ref in enumerate(suffix):
            at = slice(d * rows, (d + 1) * rows)
            keys[:, at] = ref[...]
            key_pos = ((sub_ref[0] + len(suffix) - d) % len(suffix)) * rows + iota((rows, rows), 1)
            allowed = (key_pos >= start) & (key_pos <= pos)
            floor = jnp.where(allowed, 0.0, FLOOR_SCORE)
            for h in range(heads):
                mask[h * rows : (h + 1) * rows, at] = floor

    queries = dot(normed_ref[...], wq_ref[...]).astype(BF16)
    cos_part = angle_ref[:, :half]
    sin_part = angle_ref[:, half:]
    for h in range(heads):
        base = h * (nope + rope)
        query_ref[h, :, :lat] = dot(queries[:, base : base + nope], wk_ref[h]).astype(BF16)
        first = queries[:, base + nope : base + nope + half].astype(F32)
        second = queries[:, base + nope + half : base + nope + rope].astype(F32)
        query_ref[h, :, lat:] = jnp.concatenate(
            [first * cos_part - second * sin_part, second * cos_part + first * sin_part], axis=1
        ).astype(BF16)
    scores = dot(query_ref[...].reshape(count, lat + rope), keys[...]) + mask[...]
    row_top = jnp.max(scores, axis=1, keepdims=True)
    weights = jnp.exp2((scores - row_top) * score_scale)
    denominator = jnp.sum(weights, axis=1, keepdims=True)
    weighted_ref[...] = dot_nt(weights.astype(BF16), keys[:lat])
    stats_ref[...] = jnp.where(iota(stats_ref.shape, 1) == 0, row_top, denominator)


PAIR = 2


def attend_kernel(
    score_scale, query_hbm, late_hbm, stats_hbm, near_ref, far_ref, gain_ref,
    wv_hbm, wo_hbm, tokens_hbm, place_hbm,
    residual_hbm, mid_hbm, out_hbm,
    keys, query_ref, late_ref, stats_ref, wv_ref, wo_ref, tokens_ref, place_ref,
    residual_ref, mid_ref, out_ref, sems,
):
    copies = [
        pltpu.make_async_copy(src, dst, sems.at[i])
        for i, (src, dst) in enumerate((
            (query_hbm, query_ref), (stats_hbm, stats_ref), (late_hbm, late_ref), (wv_hbm, wv_ref),
            (wo_hbm, wo_ref), (tokens_hbm, tokens_ref), (place_hbm.at[0], place_ref),
        ))
    ]
    for copy in copies:
        copy.start()
    rows = tokens_ref.shape[0]
    heads, lat, _ = wv_ref.shape
    width = query_ref.shape[2]
    near_tiles = near_ref.shape[0]
    for i in range(near_tiles):
        keys[:, i * rows : (i + 1) * rows] = near_ref[i]
        keys[:, (near_tiles + i) * rows : (near_tiles + i + 1) * rows] = far_ref[i]
    count = PAIR * rows

    def score(i):
        query = query_ref[i * PAIR : (i + 1) * PAIR].reshape(count, width)
        return dot(query, keys[...])

    def attend(i, early):
        at = slice(i * count, (i + 1) * count)
        late_top = stats_ref[at, 0:1]
        row_top = jnp.maximum(jnp.max(early, axis=1, keepdims=True), late_top)
        early = jnp.exp2((early - row_top) * score_scale)
        share = jnp.exp2((late_top - row_top) * score_scale)
        denominator = jnp.sum(early, axis=1, keepdims=True) + share * stats_ref[at, 1:2]
        weighted = dot_nt(early.astype(BF16), keys[:lat]) + late_ref[at] * share
        return (weighted / denominator).astype(BF16)

    latent_out = []
    copies[0].wait()
    current = score(0)
    copies[1].wait()
    copies[2].wait()
    for i in range(heads // PAIR):
        following = score(i + 1) if i + 1 < heads // PAIR else None
        latent_out.append(attend(i, current))
        current = following
    copies[3].wait()
    head_out = jnp.concatenate(
        [
            dot(latent_out[h // PAIR][h % PAIR * rows : (h % PAIR + 1) * rows], wv_ref[h]).astype(BF16)
            for h in range(heads)
        ],
        axis=1,
    )
    copies[4].wait()
    copies[5].wait()
    x = tokens_ref[...].astype(F32) + dot(head_out, wo_ref[...])
    residual_ref[...] = x
    base = len(copies)
    writes = [pltpu.make_async_copy(residual_ref, residual_hbm, sems.at[base])]
    writes[0].start()
    scale = lax.rsqrt(jnp.mean(x * x, axis=-1, keepdims=True) + EPSILON)
    mid = (x * scale * gain_ref[...]).astype(BF16)
    mid_ref[...] = mid
    writes.append(pltpu.make_async_copy(mid_ref, mid_hbm, sems.at[base + 1]))
    writes[1].start()
    copies[6].wait()
    step = out_ref.shape[0] // 2
    for i in range(2):
        at = slice(i * step, (i + 1) * step)
        out_ref[at] = dot(place_ref[at], mid).astype(BF16)
        writes.append(
            pltpu.make_async_copy(out_ref.at[at], out_hbm.at[at], sems.at[base + 2 + i])
        )
        writes[-1].start()
    for write in writes:
        write.wait()


def place_kernel(place_ref, mid_ref, out_ref):
    out_ref[...] = dot(place_ref[...], mid_ref[...]).astype(BF16)


def expert_kernel(x_ref, g0, u0, d0, g1, u1, d1, out_ref, buf, activated, sems):
    copies = [
        pltpu.make_async_copy(src, buf.at[i], sems.at[i])
        for i, src in enumerate((g0, u0, g1, u1, d0, d1))
    ]
    for copy in copies:
        copy.start()
    step = 256
    blocks = x_ref.shape[0] // step
    for half in range(2):
        copies[2 * half].wait()
        copies[2 * half + 1].wait()

        @pl.loop(0, blocks)
        def _(i):
            at = pl.ds(pl.multiple_of(i * step, step), step)
            gate = dot_nt(x_ref[at], buf[2 * half])
            up = dot_nt(x_ref[at], buf[2 * half + 1])
            activated[half, at] = (gate / (1.0 + jnp.exp(-gate)) * up).astype(BF16)

    copies[4].wait()
    copies[5].wait()

    @pl.loop(0, blocks)
    def _(i):
        at = pl.ds(pl.multiple_of(i * step, step), step)
        total = dot(activated[0, at], buf[4])
        out_ref[at] = (total + dot(activated[1, at], buf[5])).astype(BF16)


def mix_kernel(base_hbm, mix_hbm, rows_ref, out_hbm, base_ref, mix_ref, out_ref, sems):
    rows, model = base_ref.shape
    mix_copy = pltpu.make_async_copy(mix_hbm, mix_ref, sems.at[0])
    base_copy = pltpu.make_async_copy(base_hbm, base_ref, sems.at[1])
    mix_copy.start()
    base_copy.start()
    blocks = 4
    writes = []
    mix_copy.wait()
    for i in range(blocks):
        at = slice(i * model // blocks, (i + 1) * model // blocks)
        both = dot(mix_ref[...], rows_ref[:, at])
        if i == 0:
            base_copy.wait()
        out_ref[:, at] = (base_ref[:, at] + (both[:rows] + both[rows:])).astype(out_ref.dtype)
        writes.append(
            pltpu.make_async_copy(out_ref.at[:, at], out_hbm.at[:, at], sems.at[2 + i])
        )
        writes[-1].start()
    for write in writes:
        write.wait()


def cost(flops, moved):
    return pl.CostEstimate(flops=int(flops), bytes_accessed=int(moved), transcendentals=0)


SMEM = pl.BlockSpec(memory_space=pltpu.SMEM)
VMEM = pl.BlockSpec(memory_space=pltpu.VMEM)
HBM = pl.BlockSpec(memory_space=pltpu.HBM)


def near_core(x):
    return pltpu.with_memory_space_constraint(x, pltpu.VMEM)


def limit(mebibytes):
    return pltpu.CompilerParams(vmem_limit_bytes=mebibytes << 20)


def whole(array):
    return pl.BlockSpec(array.shape, lambda *_: (0,) * array.ndim)


def layer(
    tokens, attn_gain, w_query, w_latent, latent_gain, w_key_up, w_value_up, w_out, moe_gain,
    w_gate, w_up, w_down, expert_ids, gate_weights, lengths, slab_group, owners, prefix_pool,
):
    rows, model = tokens.shape
    head_count, nope, lat = w_key_up.shape
    width = w_latent.shape[1]
    rope = width - lat
    prefix_len = prefix_pool.shape[1]
    hidden = w_down.shape[1]
    top = expert_ids.shape[1]
    req_count = lax.axis_size("req")
    core_count = lax.axis_size("core")
    sub_count = lax.axis_size("ylo") * core_count
    chips = req_count * lax.axis_size("ylo")
    sub = lax.axis_index("ylo") * core_count + lax.axis_index("core")
    place_info = jnp.reshape(sub, (1,)).astype(jnp.int32)

    quarter_len = prefix_len // sub_count
    lanes = 128
    piece = width * quarter_len // lanes // req_count
    packed = pl.pallas_call(
        pack_kernel,
        name="pack",
        in_specs=[SMEM, SMEM, HBM],
        out_specs=VMEM,
        out_shape=pltpu.HBM((req_count, piece + (-piece % 8 or 8), lanes), BF16),
        scratch_shapes=[pltpu.VMEM((width, quarter_len), BF16), pltpu.SemaphoreType.DMA],
    )(place_info, slab_group, prefix_pool[0].T)
    spread = lax.all_to_all(
        packed, "req", split_axis=0, concat_axis=0, tiled=True
    )
    ylo_count = lax.axis_size("ylo")
    groups = spread[:, piece, 0].astype(jnp.int32)
    slots = jnp.sum(
        jnp.where(
            groups[:, None] == jnp.arange(owners.shape[0], dtype=jnp.int32)[None, :], owners[None, :], 0
        ),
        axis=1,
    )
    picked = jnp.take(spread, jnp.repeat(slots, ylo_count), axis=0, mode="clip")
    near = lax.all_to_all(picked, CHIP, split_axis=0, concat_axis=0, tiled=True)
    near = near[:, :piece].reshape(req_count, ylo_count, piece, lanes).transpose(1, 0, 2, 3)
    near = near.reshape(ylo_count * quarter_len // lanes, width, lanes)
    swap = [(0, 1), (1, 0)]
    far = lax.ppermute(near, "core", swap)

    gate_t = w_gate[0].T
    up_t = w_up[0].T
    down = w_down[0]
    gate_far = lax.ppermute(gate_t, "core", swap)
    up_far = lax.ppermute(up_t, "core", swap)
    down_far = lax.ppermute(down, "core", swap)

    pair = 2
    steps = head_count // pair
    inverse = (10000.0 ** (-np.arange(rope // 2) / (rope // 2))).astype(np.float32)
    inverse = jnp.asarray(np.ascontiguousarray(np.broadcast_to(inverse[:, None], (rope // 2, rows))))
    w_latent_t = w_latent.T
    gain_row = attn_gain[None, :]
    lgain_row = latent_gain[None, :]
    cache_t, normed, angle = pl.pallas_call(
        functools.partial(cache_kernel, prefix_len),
        name="cache",
        in_specs=[SMEM, SMEM, VMEM, VMEM, HBM, VMEM, VMEM],
        out_specs=[VMEM, VMEM, VMEM],
        out_shape=[
            pltpu.HBM((width, rows), BF16),
            pltpu.HBM((rows, model), BF16),
            pltpu.HBM((rows, rope), F32),
        ],
        scratch_shapes=[pltpu.VMEM((width, model), BF16), pltpu.SemaphoreType.DMA],
        cost_estimate=cost(2 * rows * model * width, 4e6),
    )(lengths, place_info, tokens, gain_row, w_latent_t, lgain_row, inverse)
    back = [
        lax.ppermute(cache_t, ("ylo", "core"), [(k, (k + d) % sub_count) for k in range(sub_count)])
        for d in range(1, sub_count)
    ]

    score_scale = (nope + rope) ** (-0.5) * math.log2(math.e)
    lines = head_count * rows
    query_full, late, stats = pl.pallas_call(
        functools.partial(query_kernel, score_scale),
        name="query",
        grid=(steps,),
        in_specs=[
            SMEM, SMEM, whole(normed), whole(angle),
            pl.BlockSpec((model, pair * (nope + rope)), lambda i: (0, i)),
            pl.BlockSpec((pair, nope, lat), lambda i: (i, 0, 0)),
            VMEM, VMEM, VMEM, VMEM,
        ],
        out_specs=[
            pl.BlockSpec((pair, rows, width), lambda i: (i, 0, 0)),
            pl.BlockSpec((pair * rows, lat), lambda i: (i, 0)),
            pl.BlockSpec((pair * rows, 128), lambda i: (i, 0)),
        ],
        out_shape=[
            pltpu.HBM((head_count, rows, width), BF16),
            pltpu.HBM((lines, lat), F32),
            pltpu.HBM((lines, 128), F32),
        ],
        scratch_shapes=[
            pltpu.VMEM((width, rows * sub_count), BF16),
            pltpu.VMEM((pair * rows, rows * sub_count), F32),
        ],
        compiler_params=limit(54),
        cost_estimate=cost(3e9, 12e6),
    )(
        lengths, place_info, normed, angle, w_query, w_key_up, cache_t, *map(near_core, back),
    )

    slot_count = 4 * rows * top // 3
    part_slots = slot_count // PARTS
    depth = part_slots // chips
    ids_t = expert_ids.T
    gates_t = gate_weights.T
    placing = pl.pallas_call(
        functools.partial(route_kernel, depth),
        name="route",
        in_specs=[whole(ids_t)],
        out_specs=VMEM,
        out_shape=pltpu.HBM((PARTS, part_slots, rows), BF16),
        cost_estimate=cost(1e9, 2e6),
    )(ids_t)
    mixing = []
    for part in range(PARTS):
        mixing.append(pl.pallas_call(
            functools.partial(gate_kernel, depth, part),
            name="gates",
            in_specs=[whole(ids_t), whole(gates_t), VMEM],
            out_specs=VMEM,
            out_shape=pltpu.HBM((2 * rows, part_slots), BF16),
            cost_estimate=cost(1e9, 2e6),
        )(ids_t, gates_t, placing))

    moe_row = moe_gain[None, :]
    residual, mid, first_out = pl.pallas_call(
        functools.partial(attend_kernel, score_scale),
        name="attend",
        in_specs=[HBM] * 3 + [VMEM] * 3 + [HBM] * 4,
        out_specs=[HBM, HBM, HBM],
        out_shape=[
            pltpu.HBM((rows, model), F32),
            pltpu.HBM((rows, model), BF16),
            pltpu.HBM((part_slots, model), BF16),
        ],
        scratch_shapes=[
            pltpu.VMEM((width, prefix_len), BF16),
            pltpu.VMEM(query_full.shape, BF16),
            pltpu.VMEM((lines, lat), F32),
            pltpu.VMEM((lines, 128), F32),
            pltpu.VMEM(w_value_up.shape, BF16),
            pltpu.VMEM(w_out.shape, BF16),
            pltpu.VMEM(tokens.shape, BF16),
            pltpu.VMEM((part_slots, rows), BF16),
            pltpu.VMEM((rows, model), F32),
            pltpu.VMEM((rows, model), BF16),
            pltpu.VMEM((part_slots, model), BF16),
            pltpu.SemaphoreType.DMA((11,)),
        ],
        compiler_params=limit(54),
        cost_estimate=cost(5e9, 6e6),
    )(
        query_full, late, stats, near_core(near), near_core(far),
        moe_row, w_value_up, w_out, tokens, placing,
    )

    def exchange(x):
        x = x.reshape(chips, depth, model)
        x = lax.all_to_all(x, CHIP, split_axis=0, concat_axis=0, tiled=True)
        return x.reshape(part_slots, model)

    def place(part):
        return pl.pallas_call(
            place_kernel,
            name="place",
            grid=(2,),
            in_specs=[
                pl.BlockSpec((None, part_slots // 2, rows), lambda i: (part, i, 0)), VMEM,
            ],
            out_specs=pl.BlockSpec((part_slots // 2, model), lambda i: (i, 0)),
            out_shape=pltpu.HBM((part_slots, model), BF16),
            cost_estimate=cost(2 * part_slots * rows * model, 3e6),
        )(placing, mid)

    def experts(x):
        return pl.pallas_call(
            expert_kernel,
            name="experts",
            in_specs=[VMEM] + [HBM] * 6,
            out_specs=pl.BlockSpec((part_slots, model), lambda: (0, 0)),
            out_shape=pltpu.HBM((part_slots, model), BF16),
            scratch_shapes=[
                pltpu.VMEM((6, hidden, model), BF16), pltpu.VMEM((2, part_slots, hidden), BF16),
                pltpu.SemaphoreType.DMA((6,)),
            ],
            compiler_params=limit(54),
            cost_estimate=cost(12 * part_slots * model * hidden, 21e6),
        )(near_core(x), gate_t, up_t, down, gate_far, up_far, down_far)

    def mix(base, part, x, last):
        shape = (rows, model)
        return pl.pallas_call(
            mix_kernel,
            name="mix",
            in_specs=[HBM, HBM, VMEM],
            out_specs=HBM,
            out_shape=pltpu.HBM(shape, BF16 if last else F32),
            scratch_shapes=[
                pltpu.VMEM(shape, F32), pltpu.VMEM((2 * rows, part_slots), BF16),
                pltpu.VMEM(shape, BF16 if last else F32), pltpu.SemaphoreType.DMA((6,)),
            ],
            compiler_params=limit(54),
            cost_estimate=cost(4 * part_slots * rows * model, 3e6),
        )(base, mixing[part], near_core(x))

    outbound = [first_out] + [place(part) for part in range(1, PARTS)]
    arrived = [exchange(x) for x in outbound]
    returned = [exchange(experts(x)) for x in arrived]
    total = residual
    for part in range(PARTS):
        total = mix(total, part, returned[part], part == PARTS - 1)
    return (total, cache_t.T)


def solution(mesh):
    split = Mesh(mesh.devices.reshape(mesh.devices.shape[0], -1, 2), ("req", "ylo", "core"))
    every = ("req", "ylo", "core")
    in_specs = (
        P(every, None), P(), P(), P(), P(), P(), P(), P(), P(),
        P(every, None, None), P(every, None, None), P(every, None, None),
        P(every, None), P(every, None), P("req", None), P("req"), P(), P("req", None, None),
    )
    out_specs = (P(every, None), P(every, None))
    return jax.shard_map(layer, mesh=split, in_specs=in_specs, out_specs=out_specs, check_vma=False)
```
